32 devices in a mesh: grp: 2 (over y), kxy: 8 (over z, x), kz: 2 (over core).
Axes of the slice: x: 2, y: 2, z: 4, core: 2. Of those that a mesh axis runs over, the one named last changes fastest.
Arguments:
- start_rotation: float32 [512, 2, 128, 128], P(('grp', 'kxy', 'kz')), parts along dimension 0, may hold values from -0.06 to 1.06
- correlations: float32 [512, 2, 2, 128, 128], P(('grp', 'kxy', 'kz')), parts along dimension 0, may hold values from -1.15 to 1.15
- neighbours: int32 [512, 2], P(('grp', 'kxy', 'kz')), parts along dimension 0, may hold values from 0 to 255, as said below
Outputs:
- rotation: float32 [512, 2, 128, 128], P(('grp', 'kxy', 'kz')), parts along dimension 0
- gradient: float32 [512, 2, 128, 128], P(('grp', 'kxy', 'kz')), parts along dimension 0
- centres: float32 [4, 128], P('grp'), parts along dimension 0
The draws below stay inside these ranges and needn't reach their ends.
There are 2 independent parts, one for each index of `grp`. The reference program is written for one: setup_inputs(seed, part) draws one part's arguments, and reference() takes and returns one part's arrays. A program takes and returns all parts, laid end to end along the dimension named above; each array names one. Nothing has to cross between parts.
Inputs may be any that keep to these rules, and one draw needn't show every extreme that they name: `neighbours`: entry (k, 0) is the index of the k-point one step further along kx on a periodic mesh of 4 kx planes, entry (k, 1) the one one step further along kz. Indices come in blocks of 16, each in an order of its own. Block B holds kx plane B // 4, ky half (B // 2) % 2 and kz slab B % 2; the kx neighbour of a point in block B lies in block (B + 4) mod (16); its kz neighbour lies in block B or in block B - B % 2 + (B + 1) % 2.
All inputs are finite; a program needn't handle non-finite values.
Results may differ from the reference program's by a relative error of at most 0.0003.
Values sent between devices are 32-bit elements; how exact they have to be, the bound alone decides.
No kernel may reach another device: no remote copies, remote signals or barrier semaphores. Data moves between devices by JAX's collectives and lax.ppermute only.
A program may use at most 192 MiB of HBM per device.

```python
import jax
import jax.numpy as jnp
from jax import lax

NB = 128
NW = 128
NS_STEPS = 3
KZD = 4
KPD = 16
NK = 256
N_KZ = 2


def draw_start_rotation(key, part):
    perturbation = jnp.clip(0.014 * jax.random.normal(key, (NK, 2, NB, NW), jnp.float32), -0.06, 0.06)
    identity = jnp.eye(NB, NW, dtype=jnp.float32)
    return perturbation + jnp.stack([identity, jnp.zeros_like(identity)])[None]


def draw_correlations(key, part):
    keys = jax.random.split(key, 4)
    blocks_all = NK // KPD
    ramp_factor = 1.0 + 2.0 * (jnp.arange(NK) // KPD).astype(jnp.float32) / max(blocks_all - 1, 1)
    off_diagonal = jnp.clip(0.03 * jax.random.normal(keys[0], (NK, 2, 2, NB, NB), jnp.float32), -0.15, 0.15)
    magnitude = jax.random.uniform(keys[1], (NK, 2, NB), jnp.float32, 0.6, 1.0)
    base_phase = jax.random.uniform(keys[2], (2, NB), jnp.float32, -0.3, 0.3)
    wobble = jax.random.uniform(keys[3], (NK, 2, NB), jnp.float32, -0.25, 0.25)
    phase = ramp_factor[:, None, None] * (base_phase[None] + wobble)
    diagonal = jnp.stack([magnitude * jnp.cos(phase), magnitude * jnp.sin(phase)], axis=2)
    identity = jnp.eye(NB, dtype=jnp.float32)
    return off_diagonal + diagonal[..., None, :] * identity


def draw_neighbours(key, part):
    blocks_all = NK // KPD
    orders = jax.vmap(lambda single: jax.random.permutation(single, KPD))(jax.random.split(key, blocks_all)).astype(jnp.int32)
    block_ids = jnp.arange(blocks_all, dtype=jnp.int32)
    column_ids = block_ids // N_KZ
    slab_ids = block_ids % N_KZ
    positions = jnp.arange(KPD, dtype=jnp.int32)
    row_ids = positions // KZD
    depth_ids = positions % KZD
    plane_block = (block_ids + 2 * N_KZ) % blocks_all
    plane_target = plane_block[:, None] * KPD + orders[plane_block]
    inside = (depth_ids + 1 < KZD)[None, :]
    slab_block = jnp.where(inside, block_ids[:, None], (column_ids * N_KZ + (slab_ids + 1) % N_KZ)[:, None])
    slab_pos = jnp.where(inside, (positions + 1)[None, :], (row_ids * KZD)[None, :])
    slab_target = slab_block * KPD + orders[slab_block, slab_pos]
    rows_where = (block_ids[:, None] * KPD + orders).reshape(-1)
    values = jnp.stack([plane_target.reshape(-1), slab_target.reshape(-1)], axis=-1).astype(jnp.int32)
    return jnp.zeros((NK, 2), jnp.int32).at[rows_where].set(values)


def setup_inputs(seed: int = 0, part: int = 0) -> dict:
    key_list = jax.random.split(jax.random.key(seed), 4)
    own_keys = jax.random.split(jax.random.fold_in(key_list[3], part), 4)
    return {
        "start_rotation": draw_start_rotation(jax.random.fold_in(jax.random.fold_in(key_list[3], part), 71), part),
        "correlations": draw_correlations(jax.random.fold_in(jax.random.fold_in(key_list[3], part), 71), part),
        "neighbours": draw_neighbours(jax.random.fold_in(jax.random.fold_in(key_list[3], part), 71), part),
    }


precise = lax.Precision.HIGHEST

def complex_product(left, right):
    real_part = jnp.einsum('...ij,...jk->...ik', left[..., 0, :, :], right[..., 0, :, :], precision=precise) - jnp.einsum('...ij,...jk->...ik', left[..., 1, :, :], right[..., 1, :, :], precision=precise)
    imag_part = jnp.einsum('...ij,...jk->...ik', left[..., 0, :, :], right[..., 1, :, :], precision=precise) + jnp.einsum('...ij,...jk->...ik', left[..., 1, :, :], right[..., 0, :, :], precision=precise)
    return jnp.stack([real_part, imag_part], axis=-3)

def adjoint_product(left, right):
    real_part = jnp.einsum('...ji,...jk->...ik', left[..., 0, :, :], right[..., 0, :, :], precision=precise) + jnp.einsum('...ji,...jk->...ik', left[..., 1, :, :], right[..., 1, :, :], precision=precise)
    imag_part = jnp.einsum('...ji,...jk->...ik', left[..., 0, :, :], right[..., 1, :, :], precision=precise) - jnp.einsum('...ji,...jk->...ik', left[..., 1, :, :], right[..., 0, :, :], precision=precise)
    return jnp.stack([real_part, imag_part], axis=-3)

def polar_steps(matrix):
    squares = lax.optimization_barrier(jnp.sum(matrix * matrix, axis=(-3, -2, -1), keepdims=True))
    scale = jnp.sqrt(squares / matrix.shape[-1] + 1e-06)
    current = matrix / scale
    for iteration in range(NS_STEPS):
        current = 1.5 * current - 0.5 * complex_product(current, adjoint_product(current, current))
    return current

def rotated_parts(rotated):
    real_m = rotated[..., 0, :, :]
    imag_m = rotated[..., 1, :, :]
    diag_real = jnp.diagonal(real_m, axis1=-2, axis2=-1)
    diag_imag = jnp.diagonal(imag_m, axis1=-2, axis2=-1)
    real_r = real_m * diag_real[..., None, :] + imag_m * diag_imag[..., None, :]
    imag_r = imag_m * diag_real[..., None, :] - real_m * diag_imag[..., None, :]
    return (real_r, imag_r, diag_real * diag_real + diag_imag * diag_imag)

def flipped(matrix):
    return jnp.swapaxes(matrix, -1, -2)

def rotation_terms(real_r, imag_r):
    return (0.5 * (real_r - flipped(real_r)), 0.5 * (imag_r + flipped(imag_r)))

def gradient_terms(real_r, imag_r, weight):
    real_t = real_r * weight[..., None, :]
    imag_t = imag_r * weight[..., None, :]
    return (-0.5 * (imag_t - flipped(imag_t)), 0.5 * (real_t + flipped(real_t)))

def assemble(real_g, imag_g):
    return 4.0 * jnp.stack([lax.optimization_barrier(jnp.sum(real_g, axis=-3)), lax.optimization_barrier(jnp.sum(imag_g, axis=-3))], axis=-3)

def reference(start_rotation, correlations, neighbours):
    rotation = lax.map(polar_steps, start_rotation)

    def rotate_one(inputs):
        own, correlation_pair, links = inputs
        partner = jnp.stack([rotation[links[0]], rotation[links[1]]])
        return adjoint_product(jnp.broadcast_to(own, partner.shape), complex_product(correlation_pair, partner))
    rotated = lax.map(rotate_one, (rotation, correlations, neighbours))
    diagonals = jnp.diagonal(rotated, axis1=-2, axis2=-1)
    phases = jnp.arctan2(diagonals[:, :, 1], diagonals[:, :, 0])
    centres = -lax.optimization_barrier(jnp.sum(phases, axis=0)) / (2.0 * NK)

    def gradient_one(inputs):
        matrices, angles = inputs
        real_r, imag_r, modulus = rotated_parts(matrices)
        real_a, imag_a = rotation_terms(real_r, imag_r)
        real_b, imag_b = gradient_terms(real_r, imag_r, (angles + centres) / modulus)
        return assemble(real_a + real_b, imag_a + imag_b)
    gradient = lax.map(gradient_one, (rotated, phases))
    return (rotation, gradient, centres)
```

```python
import functools

import jax
import jax.numpy as jnp
from jax import lax
from jax.experimental import pallas as pl
from jax.experimental.pallas import tpu as pltpu
from jax.sharding import PartitionSpec as P

NS_STEPS = 3
RAW = 6
CHUNKS = (4, 4, 2)
VMEM = 48 << 20


def dot(left, right, contract):
    return lax.dot_general(left, right, ((contract), ((), ())), preferred_element_type=jnp.float32)


def split(value):
    high = value.astype(jnp.bfloat16)
    return high, (value - high.astype(jnp.float32)).astype(jnp.bfloat16)


def product(left, right, contract=((1,), (0,))):
    return dot(left[0], right[0], contract) + (
        dot(left[0], right[1], contract) + dot(left[1], right[0], contract)
    )


def both(function, pair):
    return tuple(function(half) for half in pair)


def right_form(half):
    n = half.shape[0]
    return jnp.concatenate([half, jnp.concatenate([-half[:, n:], half[:, :n]], 1)], 0)


def adjoint_right_form(half):
    n = half.shape[0]
    return jnp.concatenate([half, jnp.concatenate([half[:, n:], -half[:, :n]], 1)], 0)


def identity(n):
    rows = lax.broadcasted_iota(jnp.int32, (n, n), 0)
    return (rows == lax.broadcasted_iota(jnp.int32, (n, n), 1)).astype(jnp.float32)


def polar(pairs):
    n = pairs[0][0].shape[0]
    unit = identity(n)
    unit = jnp.concatenate([1.5 * unit, jnp.zeros_like(unit)], 1)
    current = []
    for real, imag in pairs:
        scale = 1.0 / jnp.sqrt(jnp.sum(real * real + imag * imag) / n + 1e-06)
        current.append(jnp.concatenate([real * scale, imag * scale], 1))
    for _ in range(NS_STEPS):
        left = [split(value) for value in current]
        right = [both(right_form, pair) for pair in left]
        gram = [product(a, b, ((1,), (1,))) for a, b in zip(left, right)]
        factor = [split(unit - 0.5 * value) for value in gram]
        current = [product(a, b) for a, b in zip(factor, right)]
    return current


def polar_kernel(start_ref, out_ref):
    n = start_ref.shape[-1]
    count = start_ref.shape[0]
    for i, value in enumerate(polar([(start_ref[i, 0], start_ref[i, 1]) for i in range(count)])):
        out_ref[i, 0] = value[:, :n]
        out_ref[i, 1] = value[:, n:]


def polar_call(start, step):
    block = pl.BlockSpec((step,) + start.shape[1:], lambda g: (g, 0, 0, 0))
    return pl.pallas_call(
        polar_kernel,
        grid=(start.shape[0] // step,),
        in_specs=[block],
        out_specs=block,
        out_shape=jax.ShapeDtypeStruct(start.shape, start.dtype),
        compiler_params=pltpu.CompilerParams(vmem_limit_bytes=VMEM),
        name="polar",
    )(start)


def sandwich_kernel(rotation_ref, correlation_ref, out_ref):
    for i in range(rotation_ref.shape[0]):
        left = split(jnp.concatenate([rotation_ref[i, 0].T, rotation_ref[i, 1].T], 1))
        for d in range(2):
            right = split(jnp.concatenate([correlation_ref[i, d, 0], correlation_ref[i, d, 1]], 1))
            out_ref[d, i] = product(left, both(adjoint_right_form, right))


def sandwich_call(rotation, correlations, step):
    count, _, n, _ = rotation.shape
    return pl.pallas_call(
        sandwich_kernel,
        grid=(count // step,),
        in_specs=[
            pl.BlockSpec((step, 2, n, n), lambda g: (g, 0, 0, 0)),
            pl.BlockSpec((step, 2, 2, n, n), lambda g: (g, 0, 0, 0, 0)),
        ],
        out_specs=pl.BlockSpec((2, step, n, 2 * n), lambda g: (0, g, 0, 0)),
        out_shape=jax.ShapeDtypeStruct((2, count, n, 2 * n), jnp.float32),
        compiler_params=pltpu.CompilerParams(vmem_limit_bytes=VMEM),
        name="sandwich",
    )(rotation, correlations)


def column_terms(rotated, rows_ref, i):
    n = rotated.shape[0]
    unit = identity(n)
    real = jnp.sum(rotated[:, :n] * unit, axis=0, keepdims=True)
    imag = jnp.sum(rotated[:, n:] * unit, axis=0, keepdims=True)
    phase = jnp.arctan2(imag, real)
    modulus = real * real + imag * imag
    weight_real = imag / modulus
    weight_imag = real / modulus
    rows_ref[i, 0:1] = real + phase * weight_real
    rows_ref[i, 1:2] = phase * weight_imag - imag
    rows_ref[i, 2:3] = weight_real
    rows_ref[i, 3:4] = weight_imag
    return phase


def slab_kernel(slots_ref, sandwich_ref, own_ref, received_ref, out_ref, rows_ref, total_ref):
    g = pl.program_id(0)
    step = sandwich_ref.shape[1]
    count, _, n, _ = own_ref.shape

    @pl.when(g == 0)
    def _():
        total_ref[...] = jnp.zeros_like(total_ref)

    total = jnp.zeros((1, n), jnp.float32)
    for i in range(step):
        slot = slots_ref[g * step + i]
        local = slot % count
        remote = slot >= count
        partner = [jnp.where(remote, received_ref[local, p], own_ref[local, p]) for p in range(2)]
        right = both(right_form, split(jnp.concatenate(partner, 1)))
        rotated = product(split(sandwich_ref[0, i]), right)
        out_ref[i] = rotated
        total = total + column_terms(rotated, rows_ref, i)
    total_ref[1:2] = total_ref[1:2] + total


def slab_call(slots, sandwich, own, received, step):
    _, count, n, _ = sandwich.shape
    whole = pl.BlockSpec(own.shape, lambda g, s: (0, 0, 0, 0))
    return pl.pallas_call(
        slab_kernel,
        grid_spec=pltpu.PrefetchScalarGridSpec(
            num_scalar_prefetch=1,
            grid=(count // step,),
            in_specs=[pl.BlockSpec((1, step, n, 2 * n), lambda g, s: (1, g, 0, 0)), whole, whole],
            out_specs=[
                pl.BlockSpec((step, n, 2 * n), lambda g, s: (g, 0, 0)),
                pl.BlockSpec((step, 8, n), lambda g, s: (g, 0, 0)),
                pl.BlockSpec((8, n), lambda g, s: (0, 0)),
            ],
        ),
        out_shape=[
            jax.ShapeDtypeStruct((count, n, 2 * n), jnp.float32),
            jax.ShapeDtypeStruct((count, 8, n), jnp.float32),
            jax.ShapeDtypeStruct((8, n), jnp.float32),
        ],
        compiler_params=pltpu.CompilerParams(vmem_limit_bytes=VMEM),
        name="slab",
    )(slots, sandwich, own, received)


def plane_kernel(order_ref, *refs, step, raw, earlier, carried):
    sandwich_refs, refs = refs[:step], refs[step:]
    partner_ref, refs = refs[0], refs[1:]
    total_refs, refs = refs[:earlier], refs[earlier:]
    out_ref, rows_ref, total_ref = refs[2 * carried :]
    n = partner_ref.shape[-1]
    g = pl.program_id(0)

    @pl.when(g == 0)
    def _():
        total = jnp.zeros_like(total_ref)
        for other in total_refs:
            total = total + other[...]
        total_ref[...] = total

    pairs = [(partner_ref[i, 0], partner_ref[i, 1]) for i in range(step)]
    partners = polar(pairs) if raw else [jnp.concatenate(pair, 1) for pair in pairs]
    total = jnp.zeros((1, n), jnp.float32)
    rotated = [
        product(split(sandwich_refs[i][0, 0]), both(right_form, split(partners[i]))) for i in range(step)
    ]
    for i in range(step):
        out_ref[i] = rotated[i]
        total = total + column_terms(rotated[i], rows_ref, i)
    total_ref[0:1] = total_ref[0:1] + total


def plane_call(order, sandwich, partner, first, earlier, carried, step, raw):
    _, count, n, _ = sandwich.shape
    base = first // step
    own = [
        pl.BlockSpec((1, 1, n, 2 * n), lambda g, s, i=i: (0, s[first + g * step + i], 0, 0)) for i in range(step)
    ]
    small = pl.BlockSpec((8, n), lambda g, s: (0, 0))
    anywhere = pl.BlockSpec(memory_space=pl.ANY)
    aliases = {}
    if carried:
        position = 1 + step + 1 + len(earlier)
        aliases = {position: 0, position + 1: 1}
    return pl.pallas_call(
        functools.partial(plane_kernel, step=step, raw=raw, earlier=len(earlier), carried=bool(carried)),
        grid_spec=pltpu.PrefetchScalarGridSpec(
            num_scalar_prefetch=1,
            grid=(partner.shape[0] // step,),
            in_specs=own
            + [pl.BlockSpec((step, 2, n, n), lambda g, s: (g, 0, 0, 0))]
            + [small] * len(earlier)
            + [anywhere] * len(carried),
            out_specs=[
                pl.BlockSpec((step, n, 2 * n), lambda g, s: (base + g, 0, 0)),
                pl.BlockSpec((step, 8, n), lambda g, s: (base + g, 0, 0)),
                small,
            ],
        ),
        out_shape=[
            jax.ShapeDtypeStruct((count, n, 2 * n), jnp.float32),
            jax.ShapeDtypeStruct((count, 8, n), jnp.float32),
            jax.ShapeDtypeStruct((8, n), jnp.float32),
        ],
        input_output_aliases=aliases,
        compiler_params=pltpu.CompilerParams(vmem_limit_bytes=VMEM),
        name="plane",
    )(order, *([sandwich] * step), partner, *earlier, *carried)


def gradient_kernel(slots_ref, *refs, step, everything):
    totals, refs = refs[:2], refs[2:]
    plane_refs, refs = refs[:step], refs[step:]
    plane_rows, refs = refs[:step], refs[step:]
    slab_ref, slab_rows, out_ref, centres_ref = refs
    n = slab_ref.shape[1]
    centres = (totals[0][0:2] + totals[1][0:2]) / (-2.0 * everything)
    centres_ref[...] = centres
    for i in range(step):
        real = imag = None
        for d, (matrix, rows) in enumerate(((plane_refs[i], plane_rows[i]), (slab_ref, slab_rows))):
            j = 0 if d == 0 else i
            centre = centres[d : d + 1]
            v_real = 2.0 * (rows[j, 0:1] + centre * rows[j, 2:3])
            v_imag = 2.0 * (rows[j, 1:2] + centre * rows[j, 3:4])
            m_real = matrix[j, :, :n]
            m_imag = matrix[j, :, n:]
            y_real = m_real * v_real - m_imag * v_imag
            y_imag = m_real * v_imag + m_imag * v_real
            real = y_real if d == 0 else real + y_real
            imag = y_imag if d == 0 else imag + y_imag
        out_ref[i, 0] = real - real.T
        out_ref[i, 1] = imag + imag.T


def gradient_call(slots, totals, plane, plane_rows, slab, slab_rows, everything, step):
    count, n, _ = slab.shape
    small = pl.BlockSpec((8, n), lambda g, s: (0, 0))
    picked = [
        pl.BlockSpec((1, rows, width), lambda g, s, i=i: (s[g * step + i], 0, 0))
        for rows, width in ((n, 2 * n), (8, n))
        for i in range(step)
    ]
    return pl.pallas_call(
        functools.partial(gradient_kernel, step=step, everything=everything),
        grid_spec=pltpu.PrefetchScalarGridSpec(
            num_scalar_prefetch=1,
            grid=(count // step,),
            in_specs=[small, small]
            + picked
            + [
                pl.BlockSpec((step, n, 2 * n), lambda g, s: (g, 0, 0)),
                pl.BlockSpec((step, 8, n), lambda g, s: (g, 0, 0)),
            ],
            out_specs=[
                pl.BlockSpec((step, 2, n, n), lambda g, s: (g, 0, 0, 0)),
                pl.BlockSpec((2, n), lambda g, s: (0, 0)),
            ],
        ),
        out_shape=[
            jax.ShapeDtypeStruct((count, 2, n, n), jnp.float32),
            jax.ShapeDtypeStruct((2, n), jnp.float32),
        ],
        compiler_params=pltpu.CompilerParams(vmem_limit_bytes=VMEM),
        name="gradient",
    )(slots, *totals, *([plane] * step), *([plane_rows] * step), slab, slab_rows)


def shifted(value, axis, steps):
    count = lax.axis_size(axis)
    return lax.ppermute(value, axis, [(source, (source + steps) % count) for source in range(count)])


def reduce_parts(value):
    count = lax.axis_size("kxy")
    if lax.axis_size("kz") != 2 or count & (count - 1) or count < 2:
        return lax.psum(value, ("kxy", "kz")), jnp.zeros_like(value)
    value = value + shifted(value, "kz", 1)
    distance = 1
    while True:
        other = lax.ppermute(value, "kxy", [(source, source ^ distance) for source in range(count)])
        distance *= 2
        if distance == count:
            return value, other
        value = value + other


def body(start_rotation, correlations, neighbours):
    count = start_rotation.shape[0]
    block_index = lax.axis_index("kxy") * lax.axis_size("kz") + lax.axis_index("kz")
    everything = count * lax.axis_size("kxy") * lax.axis_size("kz")
    plane_slots = neighbours[:, 0] % count
    positions = jnp.arange(count, dtype=jnp.int32)
    order = jnp.max(jnp.where(plane_slots[:, None] == positions[None], positions[:, None], 0), axis=0)
    remote = (neighbours[:, 1] // count != block_index).astype(jnp.int32)
    slab_slots = neighbours[:, 1] % count + count * remote

    received = [shifted(start_rotation[:RAW], "kxy", -2)]
    rotation = polar_call(start_rotation, 4)
    first = RAW
    bounds = []
    for size in CHUNKS:
        bounds.append((first, size))
        received.append(shifted(rotation[first : first + size], "kxy", -2))
        first += size
    from_slab = shifted(rotation, "kz", -1)
    sandwich = sandwich_call(rotation, correlations, 4)
    slab, slab_rows, slab_total = slab_call(slab_slots, sandwich, rotation, from_slab, 4)
    plane, plane_rows, total = plane_call(order, sandwich, received[0], 0, [slab_total], [], 2, True)
    for (first, size), partner in zip(bounds, received[1:]):
        plane, plane_rows, total = plane_call(
            order, sandwich, partner, first, [total], [plane, plane_rows], 2, False
        )
    gradient, centres = gradient_call(
        plane_slots, reduce_parts(total), plane, plane_rows, slab, slab_rows, everything, 4
    )
    return (rotation, gradient, centres)


def solution(mesh):
    in_specs = (
        P(("grp", "kxy", "kz"), None, None, None),
        P(("grp", "kxy", "kz"), None, None, None, None),
        P(("grp", "kxy", "kz"), None),
    )
    out_specs = (
        P(("grp", "kxy", "kz"), None, None, None),
        P(("grp", "kxy", "kz"), None, None, None),
        P("grp", None),
    )
    return jax.shard_map(body, mesh=mesh, in_specs=in_specs, out_specs=out_specs, check_vma=False)
```

```python
import functools

import jax
import jax.numpy as jnp
from jax import lax
from jax.experimental import pallas as pl
from jax.experimental.pallas import tpu as pltpu
from jax.sharding import PartitionSpec as P

NS_STEPS = 3
RAW = (8,)
CHUNKS = (6, 2)
GROUP = 4
VMEM = 32 << 20


def dot(left, right, contract):
    return lax.dot_general(left, right, ((contract), ((), ())), preferred_element_type=jnp.float32)


def split(value):
    high = value.astype(jnp.bfloat16)
    return high, (value - high.astype(jnp.float32)).astype(jnp.bfloat16)


def product(left, right, contract=((1,), (0,))):
    return dot(left[0], right[0], contract) + (
        dot(left[0], right[1], contract) + dot(left[1], right[0], contract)
    )


def both(function, pair):
    return tuple(function(half) for half in pair)


def right_form(half):
    n = half.shape[0]
    return jnp.concatenate([half, jnp.concatenate([-half[:, n:], half[:, :n]], 1)], 0)


def adjoint_right_form(half):
    n = half.shape[0]
    return jnp.concatenate([half, jnp.concatenate([half[:, n:], -half[:, :n]], 1)], 0)


def identity(n):
    rows = lax.broadcasted_iota(jnp.int32, (n, n), 0)
    return (rows == lax.broadcasted_iota(jnp.int32, (n, n), 1)).astype(jnp.float32)


def polar(pairs):
    n = pairs[0][0].shape[0]
    unit = identity(n)
    unit = jnp.concatenate([1.5 * unit, jnp.zeros_like(unit)], 1)
    current = []
    for real, imag in pairs:
        scale = 1.0 / jnp.sqrt(jnp.sum(real * real + imag * imag) / n + 1e-06)
        current.append(jnp.concatenate([real * scale, imag * scale], 1))
    for _ in range(NS_STEPS):
        left = [split(value) for value in current]
        right = [both(right_form, pair) for pair in left]
        gram = [product(a, b, ((1,), (1,))) for a, b in zip(left, right)]
        factor = [split(unit - 0.5 * value) for value in gram]
        current = [product(a, b) for a, b in zip(factor, right)]
    return current


def polar_kernel(start_ref, *refs, carried, chunks):
    out_refs, chunk_refs = refs[carried : carried + 2], refs[carried + 2 :]
    n = start_ref.shape[-1]
    step = start_ref.shape[0]
    values = polar([(start_ref[i, 0], start_ref[i, 1]) for i in range(step)])

    def store(ref, i, value):
        ref[i, 0] = value[:, :n]
        ref[i, 1] = value[:, n:]

    for i, value in enumerate(values):
        for out_ref in out_refs:
            store(out_ref, i, value)
    slot = 0
    for chunk_ref, size in zip(chunk_refs, chunks):
        for i in range(size):
            pl.when(pl.program_id(0) == slot // step)(
                functools.partial(store, chunk_ref, i, values[slot % step])
            )
            slot += 1


def polar_call(start, first, count, step, carried, chunks):
    shape = start.shape[1:]
    base = first // step
    block = pl.BlockSpec((step,) + shape, lambda g: (base + g, 0, 0, 0))
    return pl.pallas_call(
        functools.partial(polar_kernel, carried=len(carried), chunks=chunks),
        grid=(count // step,),
        in_specs=[block] + [pl.BlockSpec(memory_space=pl.ANY)] * len(carried),
        out_specs=[block, pl.BlockSpec((step,) + shape, lambda g: (g, 0, 0, 0))]
        + [pl.BlockSpec((size,) + shape, lambda g: (0, 0, 0, 0)) for size in chunks],
        out_shape=[jax.ShapeDtypeStruct((size,) + shape, start.dtype) for size in (start.shape[0], count, *chunks)],
        input_output_aliases={1: 0} if carried else {},
        compiler_params=pltpu.CompilerParams(vmem_limit_bytes=VMEM),
        name="polar",
    )(start, *carried)


def take_kernel(start_ref, *refs):
    *out_refs, sems = refs
    copies = []
    first = 0
    for i, out_ref in enumerate(out_refs):
        size = out_ref.shape[0]
        copies.append(pltpu.make_async_copy(start_ref.at[pl.ds(first, size)], out_ref, sems.at[i]))
        copies[-1].start()
        first += size
    for copy in copies:
        copy.wait()


def take_call(start, sizes):
    anywhere = pl.BlockSpec(memory_space=pl.ANY)
    return pl.pallas_call(
        take_kernel,
        in_specs=[anywhere],
        out_specs=[anywhere] * len(sizes),
        out_shape=[jax.ShapeDtypeStruct((size,) + start.shape[1:], start.dtype) for size in sizes],
        scratch_shapes=[pltpu.SemaphoreType.DMA((len(sizes),))],
        name="take",
    )(start)


def sandwich_kernel(rotation_ref, correlation_ref, *out_refs):
    for i in range(rotation_ref.shape[0]):
        left = split(jnp.concatenate([rotation_ref[i, 0].T, rotation_ref[i, 1].T], 1))
        for d in range(2):
            right = split(jnp.concatenate([correlation_ref[i, d, 0], correlation_ref[i, d, 1]], 1))
            out_refs[d][i] = product(left, both(adjoint_right_form, right))


def sandwich_call(rotation, correlations, step):
    count, _, n, _ = rotation.shape
    return pl.pallas_call(
        sandwich_kernel,
        grid=(count // step,),
        in_specs=[
            pl.BlockSpec((step, 2, n, n), lambda g: (g, 0, 0, 0)),
            pl.BlockSpec((step, 2, 2, n, n), lambda g: (g, 0, 0, 0, 0)),
        ],
        out_specs=[pl.BlockSpec((step, n, 2 * n), lambda g: (g, 0, 0))] * 2,
        out_shape=[jax.ShapeDtypeStruct((count, n, 2 * n), jnp.float32)] * 2,
        compiler_params=pltpu.CompilerParams(vmem_limit_bytes=VMEM),
        name="sandwich",
    )(rotation, correlations)


def column_terms(rotated, rows_ref, i):
    n = rotated.shape[0]
    unit = identity(n)
    real = jnp.sum(rotated[:, :n] * unit, axis=0, keepdims=True)
    imag = jnp.sum(rotated[:, n:] * unit, axis=0, keepdims=True)
    phase = jnp.arctan2(imag, real)
    modulus = real * real + imag * imag
    weight_real = imag / modulus
    weight_imag = real / modulus
    rows_ref[i, 0:1] = real + phase * weight_real
    rows_ref[i, 1:2] = phase * weight_imag - imag
    rows_ref[i, 2:3] = weight_real
    rows_ref[i, 3:4] = weight_imag
    return phase


def slab_kernel(slots_ref, before_ref, sandwich_ref, own_ref, *refs, pieces):
    piece_refs, (out_ref, rows_ref, total_ref, received_ref) = refs[:pieces], refs[pieces:]
    count, _, n, _ = own_ref.shape
    first = 0
    for piece_ref in piece_refs:
        received_ref[first : first + piece_ref.shape[0]] = piece_ref[...]
        first += piece_ref.shape[0]

    def group(g, total):
        rotated = []
        for i in range(GROUP):
            slot = slots_ref[g * GROUP + i]
            local = slot % count
            remote = slot >= count
            partner = [jnp.where(remote, received_ref[local, p], own_ref[local, p]) for p in range(2)]
            right = both(right_form, split(jnp.concatenate(partner, 1)))
            rotated.append(product(split(sandwich_ref[g * GROUP + i]), right))
        for i, matrix in enumerate(rotated):
            out_ref[g * GROUP + i] = matrix
            total = total + column_terms(matrix, rows_ref, g * GROUP + i)
        return total

    total_ref[...] = before_ref[...]
    total_ref[1:2] = lax.fori_loop(0, count // GROUP, group, jnp.zeros((1, n), jnp.float32))


def slab_call(slots, total, sandwich, own, pieces):
    count, n, _ = sandwich.shape
    whole = pl.BlockSpec(memory_space=pltpu.VMEM)
    return pl.pallas_call(
        functools.partial(slab_kernel, pieces=len(pieces)),
        in_specs=[pl.BlockSpec(memory_space=pltpu.SMEM)] + [whole] * (3 + len(pieces)),
        out_specs=[whole] * 3,
        out_shape=[
            jax.ShapeDtypeStruct((count, n, 2 * n), jnp.float32),
            jax.ShapeDtypeStruct((count, 8, n), jnp.float32),
            jax.ShapeDtypeStruct((8, n), jnp.float32),
        ],
        scratch_shapes=[pltpu.VMEM(own.shape, own.dtype)],
        compiler_params=pltpu.CompilerParams(vmem_limit_bytes=VMEM),
        name="slab",
    )(slots, total, sandwich, own, *pieces)


def plane_kernel(order_ref, sandwich_ref, partner_ref, *refs, first, raw, earlier, carried):
    total_refs, refs = refs[:earlier], refs[earlier:]
    out_ref, rows_ref, total_ref = refs[2 * carried :]
    count = partner_ref.shape[0]
    total = total_refs[0][...] if earlier else jnp.zeros_like(total_ref)
    for other in total_refs[1:]:
        total = total + other[...]
    phases = jnp.zeros((1, partner_ref.shape[-1]), jnp.float32)
    for begin in range(0, count, GROUP):
        group = range(begin, min(begin + GROUP, count))
        pairs = [(partner_ref[i, 0], partner_ref[i, 1]) for i in group]
        partners = polar(pairs) if raw else [jnp.concatenate(pair, 1) for pair in pairs]
        rotated = [
            product(split(sandwich_ref[order_ref[first + i]]), both(right_form, split(partner)))
            for i, partner in zip(group, partners)
        ]
        for i, matrix in zip(group, rotated):
            out_ref[first + i] = matrix
            phases = phases + column_terms(matrix, rows_ref, first + i)
    total_ref[...] = total
    total_ref[0:1] = total[0:1] + phases


def plane_call(order, sandwich, partner, first, earlier, carried, raw):
    count, n, _ = sandwich.shape
    whole = pl.BlockSpec(memory_space=pltpu.VMEM)
    position = 3 + len(earlier)
    return pl.pallas_call(
        functools.partial(plane_kernel, first=first, raw=raw, earlier=len(earlier), carried=bool(carried)),
        in_specs=[pl.BlockSpec(memory_space=pltpu.SMEM)] + [whole] * (2 + len(earlier) + len(carried)),
        out_specs=[whole] * 3,
        out_shape=[
            jax.ShapeDtypeStruct((count, n, 2 * n), jnp.float32),
            jax.ShapeDtypeStruct((count, 8, n), jnp.float32),
            jax.ShapeDtypeStruct((8, n), jnp.float32),
        ],
        input_output_aliases={position: 0, position + 1: 1} if carried else {},
        compiler_params=pltpu.CompilerParams(vmem_limit_bytes=VMEM),
        name="plane",
    )(order, sandwich, partner, *earlier, *carried)


def gradient_kernel(
    slots_ref, first_ref, second_ref, plane_ref, plane_rows, slab_ref, slab_rows, out_ref, centres_ref, buffer, sems, *, everything
):
    count, n, _ = slab_ref.shape
    centres = (first_ref[0:2] + second_ref[0:2]) / (-2.0 * everything)
    centres_ref[...] = centres
    copies = []
    for i in range(count):
        real = imag = None
        for d, (j, matrix, rows) in enumerate(
            ((slots_ref[i], plane_ref, plane_rows), (i, slab_ref, slab_rows))
        ):
            centre = centres[d : d + 1]
            v_real = 2.0 * (rows[j, 0:1] + centre * rows[j, 2:3])
            v_imag = 2.0 * (rows[j, 1:2] + centre * rows[j, 3:4])
            m_real = matrix[j, :, :n]
            m_imag = matrix[j, :, n:]
            y_real = m_real * v_real - m_imag * v_imag
            y_imag = m_real * v_imag + m_imag * v_real
            real = y_real if d == 0 else real + y_real
            imag = y_imag if d == 0 else imag + y_imag
        buffer[i, 0] = real - real.T
        buffer[i, 1] = imag + imag.T
        copies.append(pltpu.make_async_copy(buffer.at[i], out_ref.at[i], sems.at[i]))
        copies[-1].start()
    for copy in copies:
        copy.wait()


def gradient_call(slots, totals, plane, plane_rows, slab, slab_rows, everything):
    count, n, _ = slab.shape
    whole = pl.BlockSpec(memory_space=pltpu.VMEM)
    return pl.pallas_call(
        functools.partial(gradient_kernel, everything=everything),
        in_specs=[pl.BlockSpec(memory_space=pltpu.SMEM)] + [whole] * 6,
        out_specs=[pl.BlockSpec(memory_space=pl.ANY), whole],
        out_shape=[
            jax.ShapeDtypeStruct((count, 2, n, n), jnp.float32),
            jax.ShapeDtypeStruct((2, n), jnp.float32),
        ],
        scratch_shapes=[pltpu.VMEM((count, 2, n, n), jnp.float32), pltpu.SemaphoreType.DMA((count,))],
        compiler_params=pltpu.CompilerParams(vmem_limit_bytes=VMEM),
        name="gradient",
    )(slots, *totals, plane, plane_rows, slab, slab_rows)


def shifted(value, axis, steps):
    count = lax.axis_size(axis)
    return lax.ppermute(value, axis, [(source, (source + steps) % count) for source in range(count)])


def reduce_parts(value):
    count = lax.axis_size("kxy")
    if lax.axis_size("kz") != 2 or count & (count - 1) or count < 2:
        return lax.psum(value, ("kxy", "kz")), jnp.zeros_like(value)
    value = value + shifted(value, "kz", 1)
    distance = 1
    while True:
        other = lax.ppermute(value, "kxy", [(source, source ^ distance) for source in range(count)])
        distance *= 2
        if distance == count:
            return value, other
        value = value + other


def body(start_rotation, correlations, neighbours):
    count = start_rotation.shape[0]
    block_index = lax.axis_index("kxy") * lax.axis_size("kz") + lax.axis_index("kz")
    everything = count * lax.axis_size("kxy") * lax.axis_size("kz")
    plane_slots = neighbours[:, 0] % count
    positions = jnp.arange(count, dtype=jnp.int32)
    order = jnp.max(jnp.where(plane_slots[:, None] == positions[None], positions[:, None], 0), axis=0)
    remote = (neighbours[:, 1] // count != block_index).astype(jnp.int32)
    slab_slots = neighbours[:, 1] % count + count * remote

    received = []
    first = 0
    for part in take_call(start_rotation, RAW):
        received.append((first, True, shifted(part, "kxy", -2)))
        first += part.shape[0]
    rotation, late, *parts = polar_call(start_rotation, first, count - first, GROUP, [], CHUNKS)
    for part in parts:
        received.append((first, False, shifted(part, "kxy", -2)))
        first += part.shape[0]
    rotation, early = polar_call(start_rotation, 0, sum(RAW), GROUP, [rotation], ())
    from_slab = [shifted(part, "kz", -1) for part in (early, late)]
    for_plane, for_slab = sandwich_call(rotation, correlations, 4)
    total, carried = None, []
    for first, raw, partner in received:
        earlier = [] if total is None else [total]
        plane, plane_rows, total = plane_call(order, for_plane, partner, first, earlier, carried, raw)
        if not carried:
            slab, slab_rows, total = slab_call(slab_slots, total, for_slab, rotation, from_slab)
        carried = [plane, plane_rows]
    gradient, centres = gradient_call(
        plane_slots, reduce_parts(total), plane, plane_rows, slab, slab_rows, everything
    )
    return (rotation, gradient, centres)


def solution(mesh):
    in_specs = (
        P(("grp", "kxy", "kz"), None, None, None),
        P(("grp", "kxy", "kz"), None, None, None, None),
        P(("grp", "kxy", "kz"), None),
    )
    out_specs = (
        P(("grp", "kxy", "kz"), None, None, None),
        P(("grp", "kxy", "kz"), None, None, None),
        P("grp", None),
    )
    return jax.shard_map(body, mesh=mesh, in_specs=in_specs, out_specs=out_specs, check_vma=False)
```

```python
import functools

import jax
import jax.numpy as jnp
from jax import lax
from jax.experimental import pallas as pl
from jax.experimental.pallas import tpu as pltpu
from jax.sharding import PartitionSpec as P

NS_STEPS = 3
RAW = 8
CHUNKS = (6, 2)
GROUP = 4
VMEM = 32 << 20


def dot(left, right, contract):
    return lax.dot_general(left, right, ((contract), ((), ())), preferred_element_type=jnp.float32)


def split(value):
    high = value.astype(jnp.bfloat16)
    return high, (value - high.astype(jnp.float32)).astype(jnp.bfloat16)


def product(left, right, contract=((1,), (0,))):
    return dot(left[0], right[0], contract) + (
        dot(left[0], right[1], contract) + dot(left[1], right[0], contract)
    )


def both(function, pair):
    return tuple(function(half) for half in pair)


def right_form(half):
    n = half.shape[0]
    return jnp.concatenate([half, jnp.concatenate([-half[:, n:], half[:, :n]], 1)], 0)


def adjoint_right_form(half):
    n = half.shape[0]
    return jnp.concatenate([half, jnp.concatenate([half[:, n:], -half[:, :n]], 1)], 0)


def identity(n):
    rows = lax.broadcasted_iota(jnp.int32, (n, n), 0)
    return (rows == lax.broadcasted_iota(jnp.int32, (n, n), 1)).astype(jnp.float32)


def polar(pairs):
    n = pairs[0][0].shape[0]
    unit = identity(n)
    unit = jnp.concatenate([1.5 * unit, jnp.zeros_like(unit)], 1)
    current = []
    for real, imag in pairs:
        scale = 1.0 / jnp.sqrt(jnp.sum(real * real + imag * imag) / n + 1e-06)
        current.append(jnp.concatenate([real * scale, imag * scale], 1))
    for _ in range(NS_STEPS):
        left = [split(value) for value in current]
        right = [both(right_form, pair) for pair in left]
        gram = [product(a, b, ((1,), (1,))) for a, b in zip(left, right)]
        factor = [split(unit - 0.5 * value) for value in gram]
        current = [product(a, b) for a, b in zip(factor, right)]
    return current


def polar_kernel(start_ref, *refs, carried, chunks):
    out_refs, chunk_refs = refs[carried : carried + 2], refs[carried + 2 :]
    n = start_ref.shape[-1]
    step = start_ref.shape[0]
    values = polar([(start_ref[i, 0], start_ref[i, 1]) for i in range(step)])

    def store(ref, i, value):
        ref[i, 0] = value[:, :n]
        ref[i, 1] = value[:, n:]

    for i, value in enumerate(values):
        for out_ref in out_refs:
            store(out_ref, i, value)
    slot = 0
    for chunk_ref, size in zip(chunk_refs, chunks):
        for i in range(size):
            pl.when(pl.program_id(0) == slot // step)(
                functools.partial(store, chunk_ref, i, values[slot % step])
            )
            slot += 1


def polar_call(start, first, count, step, carried, chunks):
    shape = start.shape[1:]
    base = first // step
    block = pl.BlockSpec((step,) + shape, lambda g: (base + g, 0, 0, 0))
    return pl.pallas_call(
        functools.partial(polar_kernel, carried=len(carried), chunks=chunks),
        grid=(count // step,),
        in_specs=[block] + [pl.BlockSpec(memory_space=pl.ANY)] * len(carried),
        out_specs=[block, pl.BlockSpec((step,) + shape, lambda g: (g, 0, 0, 0))]
        + [pl.BlockSpec((size,) + shape, lambda g: (0, 0, 0, 0)) for size in chunks],
        out_shape=[jax.ShapeDtypeStruct((size,) + shape, start.dtype) for size in (start.shape[0], count, *chunks)],
        input_output_aliases={1: 0} if carried else {},
        compiler_params=pltpu.CompilerParams(vmem_limit_bytes=VMEM),
        name="polar",
    )(start, *carried)


def take_kernel(start_ref, out_ref, sem):
    copy = pltpu.make_async_copy(start_ref.at[pl.ds(0, out_ref.shape[0])], out_ref, sem)
    copy.start()
    copy.wait()


def take_call(start, size):
    return pl.pallas_call(
        take_kernel,
        in_specs=[pl.BlockSpec(memory_space=pltpu.HBM)],
        out_specs=pl.BlockSpec(memory_space=pltpu.VMEM),
        out_shape=jax.ShapeDtypeStruct((size,) + start.shape[1:], start.dtype),
        scratch_shapes=[pltpu.SemaphoreType.DMA],
        compiler_params=pltpu.CompilerParams(vmem_limit_bytes=VMEM),
        name="take",
    )(start)


def sandwich_kernel(rotation_ref, correlation_ref, *out_refs):
    for i in range(rotation_ref.shape[0]):
        left = split(jnp.concatenate([rotation_ref[i, 0].T, rotation_ref[i, 1].T], 1))
        for d in range(2):
            right = split(jnp.concatenate([correlation_ref[i, d, 0], correlation_ref[i, d, 1]], 1))
            out_refs[d][i] = product(left, both(adjoint_right_form, right))


def sandwich_call(rotation, correlations, step):
    count, _, n, _ = rotation.shape
    return pl.pallas_call(
        sandwich_kernel,
        grid=(count // step,),
        in_specs=[
            pl.BlockSpec((step, 2, n, n), lambda g: (g, 0, 0, 0)),
            pl.BlockSpec((step, 2, 2, n, n), lambda g: (g, 0, 0, 0, 0)),
        ],
        out_specs=[pl.BlockSpec((step, n, 2 * n), lambda g: (g, 0, 0))] * 2,
        out_shape=[jax.ShapeDtypeStruct((count, n, 2 * n), jnp.float32)] * 2,
        compiler_params=pltpu.CompilerParams(vmem_limit_bytes=VMEM),
        name="sandwich",
    )(rotation, correlations)


def column_terms(rotated):
    n = rotated.shape[0]
    unit = identity(n)
    real = jnp.sum(rotated[:, :n] * unit, axis=0, keepdims=True)
    imag = jnp.sum(rotated[:, n:] * unit, axis=0, keepdims=True)
    phase = jnp.arctan2(imag, real)
    modulus = real * real + imag * imag
    w_real = imag / modulus
    w_imag = real / modulus
    return phase, (real + phase * w_real, phase * w_imag - imag, w_real, w_imag)


def store_rows(rows_ref, i, rows):
    for r, row in enumerate(rows):
        rows_ref[i, r : r + 1] = row


def load_rows(rows_ref, i):
    return [rows_ref[i, r : r + 1] for r in range(4)]


def scaled(matrix, v_real, v_imag):
    n = matrix.shape[0]
    real, imag = matrix[:, :n], matrix[:, n:]
    return real * v_real - imag * v_imag, real * v_imag + imag * v_real


def combine(parts_ref, slot, matrices, rows):
    real, imag = (
        sum(pair) for pair in zip(*(scaled(m, 2.0 * r[0], 2.0 * r[1]) for m, r in zip(matrices, rows)))
    )
    parts_ref[slot, 0] = real - real.T
    parts_ref[slot, 1] = imag + imag.T
    for d in range(2):
        real, imag = scaled(matrices[d], 2.0 * rows[d][2], 2.0 * rows[d][3])
        parts_ref[slot, 2 + 4 * d] = real
        parts_ref[slot, 3 + 4 * d] = imag
        parts_ref[slot, 4 + 4 * d] = real.T
        parts_ref[slot, 5 + 4 * d] = imag.T


def slab_kernel(
    order_ref, slots_ref, before_ref, plane_ref, plane_rows, sandwich_ref, own_ref, *refs, pieces
):
    piece_refs, (out_ref, rows_ref, parts_ref, total_ref, received_ref) = refs[:pieces], refs[pieces:]
    count, _, n, _ = own_ref.shape
    first = 0
    for piece_ref in piece_refs:
        received_ref[first : first + piece_ref.shape[0]] = piece_ref[...]
        first += piece_ref.shape[0]

    def group(g, total):
        rotated = []
        for i in range(GROUP):
            slot = slots_ref[g * GROUP + i]
            local = slot % count
            remote = slot >= count
            partner = [jnp.where(remote, received_ref[local, p], own_ref[local, p]) for p in range(2)]
            right = both(right_form, split(jnp.concatenate(partner, 1)))
            rotated.append(product(split(sandwich_ref[g * GROUP + i]), right))
        for i, matrix in enumerate(rotated):
            out_ref[g * GROUP + i] = matrix
            phase, rows = column_terms(matrix)
            store_rows(rows_ref, g * GROUP + i, rows)
            total = total + phase
        return total

    total_ref[...] = before_ref[...]
    total_ref[1:2] = lax.fori_loop(0, count // GROUP, group, jnp.zeros((1, n), jnp.float32))

    @pl.loop(0, plane_ref.shape[0])
    def _(slot):
        k = order_ref[slot]
        combine(
            parts_ref,
            slot,
            (plane_ref[slot], out_ref[k]),
            (load_rows(plane_rows, slot), load_rows(rows_ref, k)),
        )


def slab_call(order, slots, total, plane, plane_rows, sandwich, own, pieces):
    count, n, _ = sandwich.shape
    whole = pl.BlockSpec(memory_space=pltpu.VMEM)
    scalars = pl.BlockSpec(memory_space=pltpu.SMEM)
    return pl.pallas_call(
        functools.partial(slab_kernel, pieces=len(pieces)),
        in_specs=[scalars] * 2 + [whole] * (5 + len(pieces)),
        out_specs=[whole] * 4,
        out_shape=[
            jax.ShapeDtypeStruct((count, n, 2 * n), jnp.float32),
            jax.ShapeDtypeStruct((count, 8, n), jnp.float32),
            jax.ShapeDtypeStruct((count - CHUNKS[-1], 10, n, n), jnp.float32),
            jax.ShapeDtypeStruct((8, n), jnp.float32),
        ],
        scratch_shapes=[pltpu.VMEM(own.shape, own.dtype)],
        compiler_params=pltpu.CompilerParams(vmem_limit_bytes=VMEM),
        name="slab",
    )(order, slots, total, plane, plane_rows, sandwich, own, *pieces)


def plane_products(order_ref, sandwich_ref, partner_ref, first, raw, finish):
    count = partner_ref.shape[0]
    total = jnp.zeros((1, partner_ref.shape[-1]), jnp.float32)
    for begin in range(0, count, GROUP):
        group = range(begin, min(begin + GROUP, count))
        pairs = [(partner_ref[i, 0], partner_ref[i, 1]) for i in group]
        partners = polar(pairs) if raw else [jnp.concatenate(pair, 1) for pair in pairs]
        rotated = [
            product(split(sandwich_ref[order_ref[first + i]]), both(right_form, split(partner)))
            for i, partner in zip(group, partners)
        ]
        for i, matrix in zip(group, rotated):
            phase, rows = column_terms(matrix)
            finish(i, matrix, rows)
            total = total + phase
    return total


def plane_kernel(order_ref, sandwich_ref, partner_ref, *refs, first, raw, before):
    before_refs, (out_ref, rows_ref, total_ref) = refs[:before], refs[before:]

    def finish(i, matrix, rows):
        out_ref[i] = matrix
        store_rows(rows_ref, i, rows)

    total = plane_products(order_ref, sandwich_ref, partner_ref, first, raw, finish)
    total_ref[...] = before_refs[0][...] if before else jnp.zeros_like(total_ref)
    total_ref[0:1] = total_ref[0:1] + total


def plane_call(order, sandwich, partner, first, before, raw):
    size, _, n, _ = partner.shape
    whole = pl.BlockSpec(memory_space=pltpu.VMEM)
    return pl.pallas_call(
        functools.partial(plane_kernel, first=first, raw=raw, before=len(before)),
        in_specs=[pl.BlockSpec(memory_space=pltpu.SMEM)] + [whole] * (2 + len(before)),
        out_specs=[whole] * 3,
        out_shape=[
            jax.ShapeDtypeStruct((size, n, 2 * n), jnp.float32),
            jax.ShapeDtypeStruct((size, 8, n), jnp.float32),
            jax.ShapeDtypeStruct((8, n), jnp.float32),
        ],
        compiler_params=pltpu.CompilerParams(vmem_limit_bytes=VMEM),
        name="plane",
    )(order, sandwich, partner, *before)


def middle_kernel(
    order_ref, sandwich_ref, partner_ref, before_ref, slab_ref, slab_rows, _, parts_ref, total_ref, *, first
):
    def finish(i, matrix, rows):
        k = order_ref[first + i]
        combine(parts_ref, first + i, (matrix, slab_ref[k]), (rows, load_rows(slab_rows, k)))

    total = plane_products(order_ref, sandwich_ref, partner_ref, first, False, finish)
    total_ref[...] = before_ref[...]
    total_ref[0:1] = total_ref[0:1] + total


def middle_call(order, sandwich, partner, first, total, slab, slab_rows, parts):
    whole = pl.BlockSpec(memory_space=pltpu.VMEM)
    return pl.pallas_call(
        functools.partial(middle_kernel, first=first),
        in_specs=[pl.BlockSpec(memory_space=pltpu.SMEM)] + [whole] * 6,
        out_specs=[whole] * 2,
        out_shape=[
            jax.ShapeDtypeStruct(parts.shape, parts.dtype),
            jax.ShapeDtypeStruct(total.shape, total.dtype),
        ],
        input_output_aliases={6: 0},
        compiler_params=pltpu.CompilerParams(vmem_limit_bytes=VMEM),
        name="middle",
    )(order, sandwich, partner, total, slab, slab_rows, parts)


def gradient_kernel(
    order_ref, first_ref, second_ref, parts_ref, plane_ref, plane_rows, slab_ref, slab_rows, out_ref, centres_ref, buffer, sems, *, everything
):
    count, n, _ = slab_ref.shape
    done = parts_ref.shape[0]
    centres = (first_ref[0:2] + second_ref[0:2]) / (-2.0 * everything)
    centres_ref[...] = centres
    across = [centres[d : d + 1] for d in range(2)]
    down = [jnp.broadcast_to(row, (n, n)).T for row in across]
    copies = []

    def send(slot, real, imag):
        buffer[slot, 0] = real
        buffer[slot, 1] = imag
        copies.append(pltpu.make_async_copy(buffer.at[slot], out_ref.at[order_ref[slot]], sems.at[slot]))
        copies[-1].start()

    for slot in range(done, count):
        k = order_ref[slot]
        real = imag = jnp.zeros((n, n), jnp.float32)
        for d, (matrix, rows) in enumerate(
            ((plane_ref[slot - done], load_rows(plane_rows, slot - done)), (slab_ref[k], load_rows(slab_rows, k)))
        ):
            pair = scaled(matrix, 2.0 * (rows[0] + across[d] * rows[2]), 2.0 * (rows[1] + across[d] * rows[3]))
            real, imag = real + pair[0], imag + pair[1]
        send(slot, real - real.T, imag + imag.T)
    for slot in range(done):
        real, imag = parts_ref[slot, 0], parts_ref[slot, 1]
        for d in range(2):
            real = real + (parts_ref[slot, 2 + 4 * d] * across[d] - parts_ref[slot, 4 + 4 * d] * down[d])
            imag = imag + (parts_ref[slot, 3 + 4 * d] * across[d] + parts_ref[slot, 5 + 4 * d] * down[d])
        send(slot, real, imag)
    for copy in copies:
        copy.wait()


def gradient_call(order, totals, parts, plane, plane_rows, slab, slab_rows, everything):
    count, n, _ = slab.shape
    whole = pl.BlockSpec(memory_space=pltpu.VMEM)
    return pl.pallas_call(
        functools.partial(gradient_kernel, everything=everything),
        in_specs=[pl.BlockSpec(memory_space=pltpu.SMEM)] + [whole] * 7,
        out_specs=[pl.BlockSpec(memory_space=pl.ANY), whole],
        out_shape=[
            jax.ShapeDtypeStruct((count, 2, n, n), jnp.float32),
            jax.ShapeDtypeStruct((2, n), jnp.float32),
        ],
        scratch_shapes=[pltpu.VMEM((count, 2, n, n), jnp.float32), pltpu.SemaphoreType.DMA((count,))],
        compiler_params=pltpu.CompilerParams(vmem_limit_bytes=VMEM),
        name="gradient",
    )(order, *totals, parts, plane, plane_rows, slab, slab_rows)


def shifted(value, axis, steps):
    count = lax.axis_size(axis)
    return lax.ppermute(value, axis, [(source, (source + steps) % count) for source in range(count)])


def reduce_parts(value):
    count = lax.axis_size("kxy")
    if lax.axis_size("kz") != 2 or count & (count - 1) or count < 4:
        return lax.psum(value, ("kxy", "kz")), jnp.zeros_like(value)

    def swapped(value, bits, core):
        pairs = [(2 * s + c, 2 * (s ^ bits) + (c ^ core)) for s in range(count) for c in range(2)]
        return lax.ppermute(value, ("kxy", "kz"), pairs)

    value = value + swapped(value, 0, 1) + (swapped(value, 1, 0) + swapped(value, 1, 1))
    distance = 2
    while True:
        other = swapped(value, distance, 0)
        distance *= 2
        if distance == count:
            return value, other
        value = value + other


def body(start_rotation, correlations, neighbours):
    count = start_rotation.shape[0]
    block_index = lax.axis_index("kxy") * lax.axis_size("kz") + lax.axis_index("kz")
    everything = count * lax.axis_size("kxy") * lax.axis_size("kz")
    plane_slots = neighbours[:, 0] % count
    positions = jnp.arange(count, dtype=jnp.int32)
    order = jnp.max(jnp.where(plane_slots[:, None] == positions[None], positions[:, None], 0), axis=0)
    remote = (neighbours[:, 1] // count != block_index).astype(jnp.int32)
    slab_slots = neighbours[:, 1] % count + count * remote

    partners = [shifted(take_call(start_rotation, RAW), "kxy", -2)]
    rotation, late, *parts = polar_call(start_rotation, RAW, count - RAW, GROUP, [], CHUNKS)
    partners += [shifted(part, "kxy", -2) for part in parts]
    rotation, early = polar_call(start_rotation, 0, RAW, GROUP, [rotation], ())
    from_slab = [shifted(part, "kz", -1) for part in (early, late)]
    for_plane, for_slab = sandwich_call(rotation, correlations, GROUP)
    plane, plane_rows, total = plane_call(order, for_plane, partners[0], 0, [], True)
    slab, slab_rows, parts, total = slab_call(
        order, slab_slots, total, plane, plane_rows, for_slab, rotation, from_slab
    )
    first = RAW
    for partner in partners[1:-1]:
        parts, total = middle_call(order, for_plane, partner, first, total, slab, slab_rows, parts)
        first += partner.shape[0]
    plane, plane_rows, total = plane_call(order, for_plane, partners[-1], first, [total], False)
    gradient, centres = gradient_call(
        order, reduce_parts(total), parts, plane, plane_rows, slab, slab_rows, everything
    )
    return (rotation, gradient, centres)


def solution(mesh):
    in_specs = (
        P(("grp", "kxy", "kz"), None, None, None),
        P(("grp", "kxy", "kz"), None, None, None, None),
        P(("grp", "kxy", "kz"), None),
    )
    out_specs = (
        P(("grp", "kxy", "kz"), None, None, None),
        P(("grp", "kxy", "kz"), None, None, None),
        P("grp", None),
    )
    return jax.shard_map(body, mesh=mesh, in_specs=in_specs, out_specs=out_specs, check_vma=False)
```

```python
import functools

import jax
import jax.numpy as jnp
from jax import lax
from jax.experimental import pallas as pl
from jax.experimental.pallas import tpu as pltpu
from jax.sharding import PartitionSpec as P

NS_STEPS = 3
RAW = 8
CHUNKS = (6, 2)
GROUP = 4
VMEM = 16 << 20


def dot(left, right, contract):
    return lax.dot_general(left, right, ((contract), ((), ())), preferred_element_type=jnp.float32)


def split(value):
    high = value.astype(jnp.bfloat16)
    return high, (value - high.astype(jnp.float32)).astype(jnp.bfloat16)


def product(left, right, contract=((1,), (0,))):
    return dot(left[0], right[0], contract) + (
        dot(left[0], right[1], contract) + dot(left[1], right[0], contract)
    )


def both(function, pair):
    return tuple(function(half) for half in pair)


def right_form(half):
    n = half.shape[0]
    return jnp.concatenate([half, jnp.concatenate([-half[:, n:], half[:, :n]], 1)], 0)


def adjoint_right_form(half):
    n = half.shape[0]
    return jnp.concatenate([half, jnp.concatenate([half[:, n:], -half[:, :n]], 1)], 0)


def identity(n):
    rows = lax.broadcasted_iota(jnp.int32, (n, n), 0)
    return (rows == lax.broadcasted_iota(jnp.int32, (n, n), 1)).astype(jnp.float32)


def polar(pairs):
    n = pairs[0][0].shape[0]
    unit = identity(n)
    unit = jnp.concatenate([1.5 * unit, jnp.zeros_like(unit)], 1)
    current = []
    for real, imag in pairs:
        scale = 1.0 / jnp.sqrt(jnp.sum(real * real + imag * imag) / n + 1e-06)
        current.append(jnp.concatenate([real * scale, imag * scale], 1))
    for _ in range(NS_STEPS):
        left = [split(value) for value in current]
        right = [both(right_form, pair) for pair in left]
        gram = [product(a, b, ((1,), (1,))) for a, b in zip(left, right)]
        factor = [split(unit - 0.5 * value) for value in gram]
        current = [product(a, b) for a, b in zip(factor, right)]
    return current


def polar_kernel(start_ref, *refs, carried, chunks):
    out_refs, chunk_refs = refs[carried : carried + 2], refs[carried + 2 :]
    n = start_ref.shape[-1]
    step = start_ref.shape[0]
    values = polar([(start_ref[i, 0], start_ref[i, 1]) for i in range(step)])

    def store(ref, i, value):
        ref[i, 0] = value[:, :n]
        ref[i, 1] = value[:, n:]

    for i, value in enumerate(values):
        for out_ref in out_refs:
            store(out_ref, i, value)
    slot = 0
    for chunk_ref, size in zip(chunk_refs, chunks):
        for i in range(size):
            pl.when(pl.program_id(0) == slot // step)(
                functools.partial(store, chunk_ref, i, values[slot % step])
            )
            slot += 1


def polar_call(start, first, count, step, carried, chunks):
    shape = start.shape[1:]
    base = first // step
    block = pl.BlockSpec((step,) + shape, lambda g: (base + g, 0, 0, 0))
    return pl.pallas_call(
        functools.partial(polar_kernel, carried=len(carried), chunks=chunks),
        grid=(count // step,),
        in_specs=[block] + [pl.BlockSpec(memory_space=pl.ANY)] * len(carried),
        out_specs=[block, pl.BlockSpec((step,) + shape, lambda g: (g, 0, 0, 0))]
        + [pl.BlockSpec((size,) + shape, lambda g: (0, 0, 0, 0)) for size in chunks],
        out_shape=[jax.ShapeDtypeStruct((size,) + shape, start.dtype) for size in (start.shape[0], count, *chunks)],
        input_output_aliases={1: 0} if carried else {},
        compiler_params=pltpu.CompilerParams(vmem_limit_bytes=VMEM),
        name="polar",
    )(pltpu.with_memory_space_constraint(start, pltpu.HBM), *carried)


def take_kernel(start_ref, out_ref, sem):
    copy = pltpu.make_async_copy(start_ref.at[pl.ds(0, out_ref.shape[0])], out_ref, sem)
    copy.start()
    copy.wait()


def take_call(start, size):
    return pl.pallas_call(
        take_kernel,
        in_specs=[pl.BlockSpec(memory_space=pltpu.HBM)],
        out_specs=pl.BlockSpec(memory_space=pltpu.VMEM),
        out_shape=jax.ShapeDtypeStruct((size,) + start.shape[1:], start.dtype),
        scratch_shapes=[pltpu.SemaphoreType.DMA],
        compiler_params=pltpu.CompilerParams(vmem_limit_bytes=VMEM),
        name="take",
    )(pltpu.with_memory_space_constraint(start, pltpu.HBM))


def sandwich_kernel(rotation_ref, correlation_ref, *out_refs):
    for i in range(rotation_ref.shape[0]):
        left = split(jnp.concatenate([rotation_ref[i, 0].T, rotation_ref[i, 1].T], 1))
        for d in range(2):
            right = split(jnp.concatenate([correlation_ref[i, d, 0], correlation_ref[i, d, 1]], 1))
            out_refs[d][i] = product(left, both(adjoint_right_form, right))


def sandwich_call(rotation, correlations, step):
    count, _, n, _ = rotation.shape
    return pl.pallas_call(
        sandwich_kernel,
        grid=(count // step,),
        in_specs=[
            pl.BlockSpec((step, 2, n, n), lambda g: (g, 0, 0, 0)),
            pl.BlockSpec((step, 2, 2, n, n), lambda g: (g, 0, 0, 0, 0)),
        ],
        out_specs=[pl.BlockSpec((step, n, 2 * n), lambda g: (g, 0, 0))] * 2,
        out_shape=[jax.ShapeDtypeStruct((count, n, 2 * n), jnp.float32)] * 2,
        compiler_params=pltpu.CompilerParams(vmem_limit_bytes=VMEM),
        name="sandwich",
    )(rotation, correlations)


def column_terms(rotated):
    n = rotated.shape[0]
    unit = identity(n)
    real = jnp.sum(rotated[:, :n] * unit, axis=0, keepdims=True)
    imag = jnp.sum(rotated[:, n:] * unit, axis=0, keepdims=True)
    phase = jnp.arctan2(imag, real)
    modulus = real * real + imag * imag
    w_real = imag / modulus
    w_imag = real / modulus
    return phase, (real + phase * w_real, phase * w_imag - imag, w_real, w_imag)


def store_rows(rows_ref, i, rows):
    for r, row in enumerate(rows):
        rows_ref[i, r : r + 1] = row


def load_rows(rows_ref, i):
    return [rows_ref[i, r : r + 1] for r in range(4)]


def scaled(matrix, v_real, v_imag):
    n = matrix.shape[0]
    real, imag = matrix[:, :n], matrix[:, n:]
    return real * v_real - imag * v_imag, real * v_imag + imag * v_real


def combine(parts_ref, k, matrices, rows):
    real, imag = (
        sum(pair) for pair in zip(*(scaled(m, 2.0 * r[0], 2.0 * r[1]) for m, r in zip(matrices, rows)))
    )
    parts_ref[k, 0] = real - real.T
    parts_ref[k, 1] = imag + imag.T
    for d in range(2):
        real, imag = scaled(matrices[d], 2.0 * rows[d][2], 2.0 * rows[d][3])
        parts_ref[k, 2 + 4 * d] = real
        parts_ref[k, 3 + 4 * d] = imag
        parts_ref[k, 4 + 4 * d] = real.T
        parts_ref[k, 5 + 4 * d] = imag.T


def slab_kernel(
    order_ref, slots_ref, before_ref, plane_ref, plane_rows, sandwich_ref, own_ref, *refs, pieces
):
    piece_refs, (out_ref, rows_ref, parts_ref, total_ref, received_ref) = refs[:pieces], refs[pieces:]
    count, _, n, _ = own_ref.shape
    first = 0
    for piece_ref in piece_refs:
        received_ref[first : first + piece_ref.shape[0]] = piece_ref[...]
        first += piece_ref.shape[0]

    def group(g, total):
        rotated = []
        for i in range(GROUP):
            slot = slots_ref[g * GROUP + i]
            local = slot % count
            remote = slot >= count
            partner = [jnp.where(remote, received_ref[local, p], own_ref[local, p]) for p in range(2)]
            right = both(right_form, split(jnp.concatenate(partner, 1)))
            rotated.append(product(split(sandwich_ref[g * GROUP + i]), right))
        for i, matrix in enumerate(rotated):
            out_ref[g * GROUP + i] = matrix
            phase, rows = column_terms(matrix)
            store_rows(rows_ref, g * GROUP + i, rows)
            total = total + phase
        return total

    total_ref[...] = before_ref[...]
    total_ref[1:2] = lax.fori_loop(0, count // GROUP, group, jnp.zeros((1, n), jnp.float32))

    @pl.loop(0, plane_ref.shape[0])
    def _(slot):
        k = order_ref[slot]
        combine(
            parts_ref,
            k,
            (plane_ref[slot], out_ref[k]),
            (load_rows(plane_rows, slot), load_rows(rows_ref, k)),
        )


def slab_call(order, slots, total, plane, plane_rows, sandwich, own, pieces):
    count, n, _ = sandwich.shape
    whole = pl.BlockSpec(memory_space=pltpu.VMEM)
    scalars = pl.BlockSpec(memory_space=pltpu.SMEM)
    return pl.pallas_call(
        functools.partial(slab_kernel, pieces=len(pieces)),
        in_specs=[scalars] * 2 + [whole] * (5 + len(pieces)),
        out_specs=[whole] * 4,
        out_shape=[
            jax.ShapeDtypeStruct((count, n, 2 * n), jnp.float32),
            jax.ShapeDtypeStruct((count, 8, n), jnp.float32),
            jax.ShapeDtypeStruct((count, 10, n, n), jnp.float32),
            jax.ShapeDtypeStruct((8, n), jnp.float32),
        ],
        scratch_shapes=[pltpu.VMEM(own.shape, own.dtype)],
        compiler_params=pltpu.CompilerParams(vmem_limit_bytes=VMEM),
        name="slab",
    )(order, slots, total, plane, plane_rows, sandwich, own, *pieces)


def plane_products(partner_ref, picked, raw, finish):
    count = partner_ref.shape[0]
    total = jnp.zeros((1, partner_ref.shape[-1]), jnp.float32)
    for begin in range(0, count, GROUP):
        group = range(begin, min(begin + GROUP, count))
        pairs = [(partner_ref[i, 0], partner_ref[i, 1]) for i in group]
        partners = polar(pairs) if raw else [jnp.concatenate(pair, 1) for pair in pairs]
        rotated = [
            product(split(picked(i)), both(right_form, split(partner))) for i, partner in zip(group, partners)
        ]
        for i, matrix in zip(group, rotated):
            phase, rows = column_terms(matrix)
            finish(i, matrix, rows)
            total = total + phase
    return total


def plane_kernel(order_ref, sandwich_ref, partner_ref, before_ref, out_ref, rows_ref, total_ref, *, first):
    def finish(i, matrix, rows):
        out_ref[first + i] = matrix
        store_rows(rows_ref, first + i, rows)

    total = plane_products(partner_ref, lambda i: sandwich_ref[order_ref[first + i]], True, finish)
    total_ref[...] = before_ref[...]
    total_ref[0:1] = total_ref[0:1] + total


def plane_call(order, sandwich, partner, first, total):
    size, _, n, _ = partner.shape
    whole = pl.BlockSpec(memory_space=pltpu.VMEM)
    return pl.pallas_call(
        functools.partial(plane_kernel, first=first),
        in_specs=[pl.BlockSpec(memory_space=pltpu.SMEM)] + [whole] * 3,
        out_specs=[whole] * 3,
        out_shape=[
            jax.ShapeDtypeStruct((size, n, 2 * n), jnp.float32),
            jax.ShapeDtypeStruct((size, 8, n), jnp.float32),
            jax.ShapeDtypeStruct((8, n), jnp.float32),
        ],
        compiler_params=pltpu.CompilerParams(vmem_limit_bytes=VMEM),
        name="plane",
    )(order, sandwich, partner, total)


def middle_kernel(
    order_ref, sandwich_ref, partner_ref, before_ref, slab_ref, slab_rows, _, parts_ref, total_ref, last_ref, *, first
):
    size = partner_ref.shape[0]
    for i in range(last_ref.shape[0]):
        last_ref[i] = sandwich_ref[order_ref[first + size + i]]

    def finish(i, matrix, rows):
        k = order_ref[first + i]
        combine(parts_ref, k, (matrix, slab_ref[k]), (rows, load_rows(slab_rows, k)))

    total = plane_products(partner_ref, lambda i: sandwich_ref[order_ref[first + i]], False, finish)
    total_ref[...] = before_ref[...]
    total_ref[0:1] = total_ref[0:1] + total


def middle_call(order, sandwich, partner, first, total, slab, slab_rows, parts, last):
    _, n, width = sandwich.shape
    whole = pl.BlockSpec(memory_space=pltpu.VMEM)
    return pl.pallas_call(
        functools.partial(middle_kernel, first=first),
        in_specs=[pl.BlockSpec(memory_space=pltpu.SMEM)] + [whole] * 6,
        out_specs=[whole] * 3,
        out_shape=[
            jax.ShapeDtypeStruct(parts.shape, parts.dtype),
            jax.ShapeDtypeStruct(total.shape, total.dtype),
            jax.ShapeDtypeStruct((last, n, width), sandwich.dtype),
        ],
        input_output_aliases={6: 0},
        compiler_params=pltpu.CompilerParams(vmem_limit_bytes=VMEM),
        name="middle",
    )(order, sandwich, partner, total, slab, slab_rows, parts)


def last_kernel(sandwich_ref, partner_ref, before_ref, out_ref, rows_ref, total_ref):
    def finish(i, matrix, rows):
        out_ref[i] = matrix
        store_rows(rows_ref, i, rows)

    total = plane_products(partner_ref, lambda i: sandwich_ref[i], False, finish)
    total_ref[...] = before_ref[...]
    total_ref[0:1] = total_ref[0:1] + total


def last_call(sandwich, partner, total):
    size, n, width = sandwich.shape
    whole = pl.BlockSpec(memory_space=pltpu.VMEM)
    return pl.pallas_call(
        last_kernel,
        in_specs=[whole] * 3,
        out_specs=[whole] * 3,
        out_shape=[
            jax.ShapeDtypeStruct((size, n, width), jnp.float32),
            jax.ShapeDtypeStruct((size, 8, n), jnp.float32),
            jax.ShapeDtypeStruct(total.shape, total.dtype),
        ],
        compiler_params=pltpu.CompilerParams(vmem_limit_bytes=VMEM),
        name="last",
    )(sandwich, partner, total)


def combine_kernel(order_ref, plane_ref, plane_rows, slab_ref, slab_rows, _, parts_ref, *, first):
    for i in range(plane_ref.shape[0]):
        k = order_ref[first + i]
        combine(
            parts_ref, k, (plane_ref[i], slab_ref[k]), (load_rows(plane_rows, i), load_rows(slab_rows, k))
        )


def combine_call(order, plane, plane_rows, slab, slab_rows, parts, first):
    whole = pl.BlockSpec(memory_space=pltpu.VMEM)
    return pl.pallas_call(
        functools.partial(combine_kernel, first=first),
        in_specs=[pl.BlockSpec(memory_space=pltpu.SMEM)] + [whole] * 5,
        out_specs=whole,
        out_shape=jax.ShapeDtypeStruct(parts.shape, parts.dtype),
        input_output_aliases={5: 0},
        compiler_params=pltpu.CompilerParams(vmem_limit_bytes=VMEM),
        name="combine",
    )(order, plane, plane_rows, slab, slab_rows, parts)


def gradient_kernel(first_ref, second_ref, parts_ref, out_ref, centres_ref, buffer, small, sems, small_sem, *, everything):
    count, _, n, _ = buffer.shape
    centres = (first_ref[0:2] + second_ref[0:2]) / (-2.0 * everything)
    small[...] = centres
    small_copy = pltpu.make_async_copy(small, centres_ref, small_sem)
    small_copy.start()
    across = [centres[d : d + 1] for d in range(2)]
    down = [jnp.broadcast_to(row, (n, n)).T for row in across]

    def copy_out(k):
        return pltpu.make_async_copy(buffer.at[k], out_ref.at[k], sems.at[k])

    @pl.loop(0, count)
    def _(k):
        real, imag = parts_ref[k, 0], parts_ref[k, 1]
        for d in range(2):
            real = real + (parts_ref[k, 2 + 4 * d] * across[d] - parts_ref[k, 4 + 4 * d] * down[d])
            imag = imag + (parts_ref[k, 3 + 4 * d] * across[d] + parts_ref[k, 5 + 4 * d] * down[d])
        buffer[k, 0] = real
        buffer[k, 1] = imag
        copy_out(k).start()

    small_copy.wait()

    @pl.loop(0, count)
    def _(k):
        copy_out(k).wait()


def gradient_call(totals, parts, everything):
    count, _, n, _ = parts.shape
    whole = pl.BlockSpec(memory_space=pltpu.VMEM)
    return pl.pallas_call(
        functools.partial(gradient_kernel, everything=everything),
        in_specs=[whole] * 3,
        out_specs=[pl.BlockSpec(memory_space=pl.ANY)] * 2,
        out_shape=[
            jax.ShapeDtypeStruct((count, 2, n, n), jnp.float32),
            jax.ShapeDtypeStruct((2, n), jnp.float32),
        ],
        scratch_shapes=[
            pltpu.VMEM((count, 2, n, n), jnp.float32),
            pltpu.VMEM((2, n), jnp.float32),
            pltpu.SemaphoreType.DMA((count,)),
            pltpu.SemaphoreType.DMA,
        ],
        compiler_params=pltpu.CompilerParams(vmem_limit_bytes=VMEM),
        name="gradient",
    )(*totals, parts)


def shifted(value, axis, steps):
    count = lax.axis_size(axis)
    return lax.ppermute(value, axis, [(source, (source + steps) % count) for source in range(count)])


def reduce_parts(value):
    count = lax.axis_size("kxy")
    if lax.axis_size("kz") != 2 or count & (count - 1) or count < 4:
        return lax.psum(value, ("kxy", "kz")), jnp.zeros_like(value)

    def swapped(value, bits, core):
        pairs = [(2 * s + c, 2 * (s ^ bits) + (c ^ core)) for s in range(count) for c in range(2)]
        return lax.ppermute(value, ("kxy", "kz"), pairs)

    value = value + swapped(value, 0, 1) + (swapped(value, 1, 0) + swapped(value, 1, 1))
    distance = count // 2
    while distance > 2:
        value = value + swapped(value, distance, 1)
        distance //= 2
    return value, swapped(value, distance, 1)


def body(start_rotation, correlations, neighbours):
    count = start_rotation.shape[0]
    block_index = lax.axis_index("kxy") * lax.axis_size("kz") + lax.axis_index("kz")
    everything = count * lax.axis_size("kxy") * lax.axis_size("kz")
    plane_slots = neighbours[:, 0] % count
    positions = jnp.arange(count, dtype=jnp.int32)
    order = jnp.max(jnp.where(plane_slots[:, None] == positions[None], positions[:, None], 0), axis=0)
    remote = (neighbours[:, 1] // count != block_index).astype(jnp.int32)
    slab_slots = neighbours[:, 1] % count + count * remote

    partners = [shifted(take_call(start_rotation, RAW), "kxy", -2)]
    rotation, late, *parts = polar_call(start_rotation, RAW, count - RAW, GROUP, [], CHUNKS)
    partners += [shifted(part, "kxy", -2) for part in parts]
    rotation, early = polar_call(start_rotation, 0, RAW, GROUP, [rotation], ())
    from_slab = [shifted(part, "kz", -1) for part in (early, late)]
    for_plane, for_slab = sandwich_call(rotation, correlations, GROUP)
    total = jnp.zeros((8, rotation.shape[-1]), jnp.float32)
    plane, plane_rows, total = plane_call(order, for_plane, partners[0], 0, total)
    slab, slab_rows, parts, total = slab_call(
        order, slab_slots, total, plane, plane_rows, for_slab, rotation, from_slab
    )
    parts, total, for_last = middle_call(
        order, for_plane, partners[1], RAW, total, slab, slab_rows, parts, CHUNKS[-1]
    )
    plane, plane_rows, total = last_call(for_last, partners[2], total)
    totals = reduce_parts(total)
    parts = combine_call(order, plane, plane_rows, slab, slab_rows, parts, count - CHUNKS[-1])
    gradient, centres = gradient_call(totals, parts, everything)
    return (rotation, gradient, centres)


def solution(mesh):
    in_specs = (
        P(("grp", "kxy", "kz"), None, None, None),
        P(("grp", "kxy", "kz"), None, None, None, None),
        P(("grp", "kxy", "kz"), None),
    )
    out_specs = (
        P(("grp", "kxy", "kz"), None, None, None),
        P(("grp", "kxy", "kz"), None, None, None),
        P("grp", None),
    )
    return jax.shard_map(body, mesh=mesh, in_specs=in_specs, out_specs=out_specs, check_vma=False)
```

```python
import functools

import jax
import jax.numpy as jnp
from jax import lax
from jax.experimental import pallas as pl
from jax.experimental.pallas import tpu as pltpu
from jax.sharding import PartitionSpec as P

NS_STEPS = 3
RAW = 8
CHUNKS = (6, 2)
GROUP = 4
VMEM = 16 << 20


def dot(left, right, contract):
    return lax.dot_general(left, right, ((contract), ((), ())), preferred_element_type=jnp.float32)


def split(value):
    high = value.astype(jnp.bfloat16)
    return high, (value - high.astype(jnp.float32)).astype(jnp.bfloat16)


def product(left, right, contract=((1,), (0,))):
    return dot(left[0], right[0], contract) + (
        dot(left[0], right[1], contract) + dot(left[1], right[0], contract)
    )


def both(function, pair):
    return tuple(function(half) for half in pair)


def right_form(half):
    n = half.shape[0]
    return jnp.concatenate([half, jnp.concatenate([-half[:, n:], half[:, :n]], 1)], 0)


def adjoint_right_form(half):
    n = half.shape[0]
    return jnp.concatenate([half, jnp.concatenate([half[:, n:], -half[:, :n]], 1)], 0)


def identity(n):
    rows = lax.broadcasted_iota(jnp.int32, (n, n), 0)
    return (rows == lax.broadcasted_iota(jnp.int32, (n, n), 1)).astype(jnp.float32)


def polar(pairs):
    n = pairs[0][0].shape[0]
    unit = identity(n)
    unit = jnp.concatenate([1.5 * unit, jnp.zeros_like(unit)], 1)
    current = []
    for real, imag in pairs:
        scale = 1.0 / jnp.sqrt(jnp.sum(real * real + imag * imag) / n + 1e-06)
        current.append(jnp.concatenate([real * scale, imag * scale], 1))
    for _ in range(NS_STEPS):
        left = [split(value) for value in current]
        right = [both(right_form, pair) for pair in left]
        gram = [product(a, b, ((1,), (1,))) for a, b in zip(left, right)]
        factor = [split(unit - 0.5 * value) for value in gram]
        current = [product(a, b) for a, b in zip(factor, right)]
    return current


def polar_kernel(start_ref, *refs, carried, chunks):
    out_refs, chunk_refs = refs[carried : carried + 2], refs[carried + 2 :]
    n = start_ref.shape[-1]
    step = start_ref.shape[0]
    values = polar([(start_ref[i, 0], start_ref[i, 1]) for i in range(step)])

    def store(ref, i, value):
        ref[i, 0] = value[:, :n]
        ref[i, 1] = value[:, n:]

    for i, value in enumerate(values):
        for out_ref in out_refs:
            store(out_ref, i, value)
    slot = 0
    for chunk_ref, size in zip(chunk_refs, chunks):
        for i in range(size):
            pl.when(pl.program_id(0) == slot // step)(
                functools.partial(store, chunk_ref, i, values[slot % step])
            )
            slot += 1


def polar_call(start, first, count, step, carried, chunks):
    shape = start.shape[1:]
    base = first // step
    block = pl.BlockSpec((step,) + shape, lambda g: (base + g, 0, 0, 0))
    return pl.pallas_call(
        functools.partial(polar_kernel, carried=len(carried), chunks=chunks),
        grid=(count // step,),
        in_specs=[block] + [pl.BlockSpec(memory_space=pl.ANY)] * len(carried),
        out_specs=[block, pl.BlockSpec((step,) + shape, lambda g: (g, 0, 0, 0))]
        + [pl.BlockSpec((size,) + shape, lambda g: (0, 0, 0, 0)) for size in chunks],
        out_shape=[jax.ShapeDtypeStruct((size,) + shape, start.dtype) for size in (start.shape[0], count, *chunks)],
        input_output_aliases={1: 0} if carried else {},
        compiler_params=pltpu.CompilerParams(vmem_limit_bytes=VMEM),
        name="polar",
    )(pltpu.with_memory_space_constraint(start, pltpu.HBM), *carried)


def take_kernel(start_ref, out_ref, sem):
    copy = pltpu.make_async_copy(start_ref.at[pl.ds(0, out_ref.shape[0])], out_ref, sem)
    copy.start()
    copy.wait()


def take_call(start, size):
    return pl.pallas_call(
        take_kernel,
        in_specs=[pl.BlockSpec(memory_space=pltpu.HBM)],
        out_specs=pl.BlockSpec(memory_space=pltpu.VMEM),
        out_shape=jax.ShapeDtypeStruct((size,) + start.shape[1:], start.dtype),
        scratch_shapes=[pltpu.SemaphoreType.DMA],
        compiler_params=pltpu.CompilerParams(vmem_limit_bytes=VMEM),
        name="take",
    )(pltpu.with_memory_space_constraint(start, pltpu.HBM))


def sandwich_kernel(rotation_ref, correlation_ref, *out_refs):
    for i in range(rotation_ref.shape[0]):
        left = split(jnp.concatenate([rotation_ref[i, 0].T, rotation_ref[i, 1].T], 1))
        for d in range(2):
            right = split(jnp.concatenate([correlation_ref[i, d, 0], correlation_ref[i, d, 1]], 1))
            out_refs[d][i] = product(left, both(adjoint_right_form, right))


def sandwich_call(rotation, correlations, step):
    count, _, n, _ = rotation.shape
    return pl.pallas_call(
        sandwich_kernel,
        grid=(count // step,),
        in_specs=[
            pl.BlockSpec((step, 2, n, n), lambda g: (g, 0, 0, 0)),
            pl.BlockSpec((step, 2, 2, n, n), lambda g: (g, 0, 0, 0, 0)),
        ],
        out_specs=[pl.BlockSpec((step, n, 2 * n), lambda g: (g, 0, 0))] * 2,
        out_shape=[jax.ShapeDtypeStruct((count, n, 2 * n), jnp.float32)] * 2,
        compiler_params=pltpu.CompilerParams(vmem_limit_bytes=VMEM),
        name="sandwich",
    )(rotation, correlations)


def column_terms(rotated):
    n = rotated.shape[0]
    unit = identity(n)
    real = jnp.sum(rotated[:, :n] * unit, axis=0, keepdims=True)
    imag = jnp.sum(rotated[:, n:] * unit, axis=0, keepdims=True)
    phase = jnp.arctan2(imag, real)
    modulus = real * real + imag * imag
    w_real = imag / modulus
    w_imag = real / modulus
    return phase, (real + phase * w_real, phase * w_imag - imag, w_real, w_imag)


def store_rows(rows_ref, i, rows):
    for r, row in enumerate(rows):
        rows_ref[i, r : r + 1] = row


def load_rows(rows_ref, i):
    return [rows_ref[i, r : r + 1] for r in range(4)]


def scaled(matrix, v_real, v_imag):
    n = matrix.shape[0]
    real, imag = matrix[:, :n], matrix[:, n:]
    return real * v_real - imag * v_imag, real * v_imag + imag * v_real


def combine(parts_ref, k, matrices, rows):
    real, imag = (
        sum(pair) for pair in zip(*(scaled(m, 2.0 * r[0], 2.0 * r[1]) for m, r in zip(matrices, rows)))
    )
    parts_ref[k, 0] = real - real.T
    parts_ref[k, 1] = imag + imag.T
    for d in range(2):
        real, imag = scaled(matrices[d], 2.0 * rows[d][2], 2.0 * rows[d][3])
        parts_ref[k, 2 + 4 * d] = real
        parts_ref[k, 3 + 4 * d] = imag
        parts_ref[k, 4 + 4 * d] = real.T
        parts_ref[k, 5 + 4 * d] = imag.T


def slab_kernel(
    order_ref, slots_ref, before_ref, plane_ref, plane_rows, sandwich_ref, own_ref, *refs, pieces
):
    piece_refs, (out_ref, rows_ref, parts_ref, total_ref, received_ref) = refs[:pieces], refs[pieces:]
    count, _, n, _ = own_ref.shape
    first = 0
    for piece_ref in piece_refs:
        received_ref[first : first + piece_ref.shape[0]] = piece_ref[...]
        first += piece_ref.shape[0]

    def group(g, total):
        rotated = []
        for i in range(GROUP):
            slot = slots_ref[g * GROUP + i]
            local = slot % count
            remote = slot >= count
            partner = [jnp.where(remote, received_ref[local, p], own_ref[local, p]) for p in range(2)]
            right = both(right_form, split(jnp.concatenate(partner, 1)))
            rotated.append(product(split(sandwich_ref[g * GROUP + i]), right))
        for i, matrix in enumerate(rotated):
            out_ref[g * GROUP + i] = matrix
            phase, rows = column_terms(matrix)
            store_rows(rows_ref, g * GROUP + i, rows)
            total = total + phase
        return total

    total_ref[...] = before_ref[...]
    total_ref[1:2] = lax.fori_loop(0, count // GROUP, group, jnp.zeros((1, n), jnp.float32))

    @pl.loop(0, plane_ref.shape[0])
    def _(slot):
        k = order_ref[slot]
        combine(
            parts_ref,
            k,
            (plane_ref[slot], out_ref[k]),
            (load_rows(plane_rows, slot), load_rows(rows_ref, k)),
        )


def slab_call(order, slots, total, plane, plane_rows, sandwich, own, pieces):
    count, n, _ = sandwich.shape
    whole = pl.BlockSpec(memory_space=pltpu.VMEM)
    scalars = pl.BlockSpec(memory_space=pltpu.SMEM)
    return pl.pallas_call(
        functools.partial(slab_kernel, pieces=len(pieces)),
        in_specs=[scalars] * 2 + [whole] * (5 + len(pieces)),
        out_specs=[whole] * 4,
        out_shape=[
            jax.ShapeDtypeStruct((count, n, 2 * n), jnp.float32),
            jax.ShapeDtypeStruct((count, 8, n), jnp.float32),
            jax.ShapeDtypeStruct((count, 10, n, n), jnp.float32),
            jax.ShapeDtypeStruct((2, n), jnp.float32),
        ],
        scratch_shapes=[pltpu.VMEM(own.shape, own.dtype)],
        compiler_params=pltpu.CompilerParams(vmem_limit_bytes=VMEM),
        name="slab",
    )(order, slots, total, plane, plane_rows, sandwich, own, *pieces)


def plane_products(partner_ref, picked, raw, finish):
    count = partner_ref.shape[0]
    total = jnp.zeros((1, partner_ref.shape[-1]), jnp.float32)
    for begin in range(0, count, GROUP):
        group = range(begin, min(begin + GROUP, count))
        pairs = [(partner_ref[i, 0], partner_ref[i, 1]) for i in group]
        partners = polar(pairs) if raw else [jnp.concatenate(pair, 1) for pair in pairs]
        rotated = [
            product(split(picked(i)), both(right_form, split(partner))) for i, partner in zip(group, partners)
        ]
        for i, matrix in zip(group, rotated):
            phase, rows = column_terms(matrix)
            finish(i, matrix, rows)
            total = total + phase
    return total


def plane_kernel(order_ref, sandwich_ref, partner_ref, before_ref, out_ref, rows_ref, total_ref, *, first):
    def finish(i, matrix, rows):
        out_ref[first + i] = matrix
        store_rows(rows_ref, first + i, rows)

    total = plane_products(partner_ref, lambda i: sandwich_ref[order_ref[first + i]], True, finish)
    total_ref[...] = before_ref[...]
    total_ref[0:1] = total_ref[0:1] + total


def plane_call(order, sandwich, partner, first, total):
    size, _, n, _ = partner.shape
    whole = pl.BlockSpec(memory_space=pltpu.VMEM)
    return pl.pallas_call(
        functools.partial(plane_kernel, first=first),
        in_specs=[pl.BlockSpec(memory_space=pltpu.SMEM)] + [whole] * 3,
        out_specs=[whole] * 3,
        out_shape=[
            jax.ShapeDtypeStruct((size, n, 2 * n), jnp.float32),
            jax.ShapeDtypeStruct((size, 8, n), jnp.float32),
            jax.ShapeDtypeStruct((2, n), jnp.float32),
        ],
        compiler_params=pltpu.CompilerParams(vmem_limit_bytes=VMEM),
        name="plane",
    )(order, sandwich, partner, total)


def middle_kernel(
    order_ref, sandwich_ref, partner_ref, before_ref, slab_ref, slab_rows, _, parts_ref, total_ref, last_ref, *, first
):
    size = partner_ref.shape[0]
    for i in range(last_ref.shape[0]):
        last_ref[i] = sandwich_ref[order_ref[first + size + i]]

    def finish(i, matrix, rows):
        k = order_ref[first + i]
        combine(parts_ref, k, (matrix, slab_ref[k]), (rows, load_rows(slab_rows, k)))

    total = plane_products(partner_ref, lambda i: sandwich_ref[order_ref[first + i]], False, finish)
    total_ref[...] = before_ref[...]
    total_ref[0:1] = total_ref[0:1] + total


def middle_call(order, sandwich, partner, first, total, slab, slab_rows, parts, last):
    _, n, width = sandwich.shape
    whole = pl.BlockSpec(memory_space=pltpu.VMEM)
    return pl.pallas_call(
        functools.partial(middle_kernel, first=first),
        in_specs=[pl.BlockSpec(memory_space=pltpu.SMEM)] + [whole] * 6,
        out_specs=[whole] * 3,
        out_shape=[
            jax.ShapeDtypeStruct(parts.shape, parts.dtype),
            jax.ShapeDtypeStruct(total.shape, total.dtype),
            jax.ShapeDtypeStruct((last, n, width), sandwich.dtype),
        ],
        input_output_aliases={6: 0},
        compiler_params=pltpu.CompilerParams(vmem_limit_bytes=VMEM),
        name="middle",
    )(order, sandwich, partner, total, slab, slab_rows, parts)


def last_kernel(sandwich_ref, partner_ref, before_ref, out_ref, rows_ref, total_ref):
    def finish(i, matrix, rows):
        out_ref[i] = matrix
        store_rows(rows_ref, i, rows)

    total = plane_products(partner_ref, lambda i: sandwich_ref[i], False, finish)
    total_ref[...] = before_ref[...]
    total_ref[0:1] = total_ref[0:1] + total


def last_call(sandwich, partner, total):
    size, n, width = sandwich.shape
    whole = pl.BlockSpec(memory_space=pltpu.VMEM)
    return pl.pallas_call(
        last_kernel,
        in_specs=[whole] * 3,
        out_specs=[whole] * 3,
        out_shape=[
            jax.ShapeDtypeStruct((size, n, width), jnp.float32),
            jax.ShapeDtypeStruct((size, 8, n), jnp.float32),
            jax.ShapeDtypeStruct(total.shape, total.dtype),
        ],
        compiler_params=pltpu.CompilerParams(vmem_limit_bytes=VMEM),
        name="last",
    )(sandwich, partner, total)


def combine_kernel(order_ref, plane_ref, plane_rows, slab_ref, slab_rows, _, parts_ref, *, first):
    for i in range(plane_ref.shape[0]):
        k = order_ref[first + i]
        combine(
            parts_ref, k, (plane_ref[i], slab_ref[k]), (load_rows(plane_rows, i), load_rows(slab_rows, k))
        )


def combine_call(order, plane, plane_rows, slab, slab_rows, parts, first):
    whole = pl.BlockSpec(memory_space=pltpu.VMEM)
    return pl.pallas_call(
        functools.partial(combine_kernel, first=first),
        in_specs=[pl.BlockSpec(memory_space=pltpu.SMEM)] + [whole] * 5,
        out_specs=whole,
        out_shape=jax.ShapeDtypeStruct(parts.shape, parts.dtype),
        input_output_aliases={5: 0},
        compiler_params=pltpu.CompilerParams(vmem_limit_bytes=VMEM),
        name="combine",
    )(order, plane, plane_rows, slab, slab_rows, parts)


def gradient_kernel(first_ref, second_ref, parts_ref, out_ref, centres_ref, buffer, small, sems, small_sem, *, everything):
    count, _, n, _ = buffer.shape
    centres = (first_ref[...] + second_ref[...]) / (-2.0 * everything)
    small[...] = centres
    small_copy = pltpu.make_async_copy(small, centres_ref, small_sem)
    small_copy.start()
    across = [centres[d : d + 1] for d in range(2)]
    down = [jnp.broadcast_to(row, (n, n)).T for row in across]

    def copy_out(k):
        return pltpu.make_async_copy(buffer.at[k], out_ref.at[k], sems.at[k])

    @pl.loop(0, count)
    def _(k):
        real, imag = parts_ref[k, 0], parts_ref[k, 1]
        for d in range(2):
            real = real + (parts_ref[k, 2 + 4 * d] * across[d] - parts_ref[k, 4 + 4 * d] * down[d])
            imag = imag + (parts_ref[k, 3 + 4 * d] * across[d] + parts_ref[k, 5 + 4 * d] * down[d])
        buffer[k, 0] = real
        buffer[k, 1] = imag
        copy_out(k).start()

    small_copy.wait()

    @pl.loop(0, count)
    def _(k):
        copy_out(k).wait()


def gradient_call(totals, parts, everything):
    count, _, n, _ = parts.shape
    whole = pl.BlockSpec(memory_space=pltpu.VMEM)
    return pl.pallas_call(
        functools.partial(gradient_kernel, everything=everything),
        in_specs=[whole] * 3,
        out_specs=[pl.BlockSpec(memory_space=pl.ANY)] * 2,
        out_shape=[
            jax.ShapeDtypeStruct((count, 2, n, n), jnp.float32),
            jax.ShapeDtypeStruct((2, n), jnp.float32),
        ],
        scratch_shapes=[
            pltpu.VMEM((count, 2, n, n), jnp.float32),
            pltpu.VMEM((2, n), jnp.float32),
            pltpu.SemaphoreType.DMA((count,)),
            pltpu.SemaphoreType.DMA,
        ],
        compiler_params=pltpu.CompilerParams(vmem_limit_bytes=VMEM),
        name="gradient",
    )(*totals, parts)


def shifted(value, axis, steps):
    count = lax.axis_size(axis)
    return lax.ppermute(value, axis, [(source, (source + steps) % count) for source in range(count)])


def reduce_parts(value):
    count = lax.axis_size("kxy")
    if lax.axis_size("kz") != 2 or count & (count - 1) or count < 4:
        return lax.psum(value, ("kxy", "kz")), jnp.zeros_like(value)

    def swapped(value, bits, core):
        pairs = [(2 * s + c, 2 * (s ^ bits) + (c ^ core)) for s in range(count) for c in range(2)]
        return lax.ppermute(value, ("kxy", "kz"), pairs)

    value = value + swapped(value, 0, 1) + (swapped(value, 1, 0) + swapped(value, 1, 1))
    distance = count // 2
    while distance > 2:
        value = value + swapped(value, distance, 1)
        distance //= 2
    return value, swapped(value, distance, 1)


def body(start_rotation, correlations, neighbours):
    count = start_rotation.shape[0]
    block_index = lax.axis_index("kxy") * lax.axis_size("kz") + lax.axis_index("kz")
    everything = count * lax.axis_size("kxy") * lax.axis_size("kz")
    plane_slots = neighbours[:, 0] % count
    positions = jnp.arange(count, dtype=jnp.int32)
    order = jnp.max(jnp.where(plane_slots[:, None] == positions[None], positions[:, None], 0), axis=0)
    remote = (neighbours[:, 1] // count != block_index).astype(jnp.int32)
    slab_slots = neighbours[:, 1] % count + count * remote

    partners = [shifted(take_call(start_rotation, RAW), "kxy", -2)]
    rotation, late, *parts = polar_call(start_rotation, RAW, count - RAW, GROUP, [], CHUNKS)
    partners += [shifted(part, "kxy", -2) for part in parts]
    rotation, early = polar_call(start_rotation, 0, RAW, GROUP, [rotation], ())
    from_slab = [shifted(part, "kz", -1) for part in (early, late)]
    for_plane, for_slab = sandwich_call(rotation, correlations, GROUP)
    total = jnp.zeros((2, rotation.shape[-1]), jnp.float32)
    plane, plane_rows, total = plane_call(order, for_plane, partners[0], 0, total)
    slab, slab_rows, parts, total = slab_call(
        order, slab_slots, total, plane, plane_rows, for_slab, rotation, from_slab
    )
    parts, total, for_last = middle_call(
        order, for_plane, partners[1], RAW, total, slab, slab_rows, parts, CHUNKS[-1]
    )
    plane, plane_rows, total = last_call(for_last, partners[2], total)
    totals = reduce_parts(total)
    parts = combine_call(order, plane, plane_rows, slab, slab_rows, parts, count - CHUNKS[-1])
    gradient, centres = gradient_call(totals, parts, everything)
    return (rotation, gradient, centres)


def solution(mesh):
    in_specs = (
        P(("grp", "kxy", "kz"), None, None, None),
        P(("grp", "kxy", "kz"), None, None, None, None),
        P(("grp", "kxy", "kz"), None),
    )
    out_specs = (
        P(("grp", "kxy", "kz"), None, None, None),
        P(("grp", "kxy", "kz"), None, None, None),
        P("grp", None),
    )
    return jax.shard_map(body, mesh=mesh, in_specs=in_specs, out_specs=out_specs, check_vma=False)
```

```python
import functools

import jax
import jax.numpy as jnp
from jax import lax
from jax.experimental import pallas as pl
from jax.experimental.pallas import tpu as pltpu
from jax.sharding import PartitionSpec as P

NS_STEPS = 3
RAW = 8
CHUNKS = (6, 2)
GROUP = 4
VMEM = 16 << 20


def dot(left, right, contract):
    return lax.dot_general(left, right, ((contract), ((), ())), preferred_element_type=jnp.float32)


def split(value):
    high = value.astype(jnp.bfloat16)
    return high, (value - high.astype(jnp.float32)).astype(jnp.bfloat16)


def product(left, right, contract=((1,), (0,))):
    return dot(left[0], right[0], contract) + (
        dot(left[0], right[1], contract) + dot(left[1], right[0], contract)
    )


def both(function, pair):
    return tuple(function(half) for half in pair)


def right_form(half):
    n = half.shape[0]
    return jnp.concatenate([half, jnp.concatenate([-half[:, n:], half[:, :n]], 1)], 0)


def adjoint_right_form(half):
    n = half.shape[0]
    return jnp.concatenate([half, jnp.concatenate([half[:, n:], -half[:, :n]], 1)], 0)


def identity(n):
    rows = lax.broadcasted_iota(jnp.int32, (n, n), 0)
    return (rows == lax.broadcasted_iota(jnp.int32, (n, n), 1)).astype(jnp.float32)


def polar(pairs):
    n = pairs[0][0].shape[0]
    unit = identity(n)
    unit = jnp.concatenate([1.5 * unit, jnp.zeros_like(unit)], 1)
    current = []
    for real, imag in pairs:
        scale = 1.0 / jnp.sqrt(jnp.sum(real * real + imag * imag) / n + 1e-06)
        current.append(jnp.concatenate([real * scale, imag * scale], 1))
    for _ in range(NS_STEPS):
        left = [split(value) for value in current]
        right = [both(right_form, pair) for pair in left]
        gram = [product(a, b, ((1,), (1,))) for a, b in zip(left, right)]
        factor = [split(unit - 0.5 * value) for value in gram]
        current = [product(a, b) for a, b in zip(factor, right)]
    return current


def polar_kernel(start_ref, *refs, carried, chunks):
    out_refs, chunk_refs = refs[carried : carried + 2], refs[carried + 2 :]
    n = start_ref.shape[-1]
    step = start_ref.shape[0]
    values = polar([(start_ref[i, 0], start_ref[i, 1]) for i in range(step)])

    def store(ref, i, value):
        ref[i, 0] = value[:, :n]
        ref[i, 1] = value[:, n:]

    for i, value in enumerate(values):
        for out_ref in out_refs:
            store(out_ref, i, value)
    slot = 0
    for chunk_ref, size in zip(chunk_refs, chunks):
        for i in range(size):
            pl.when(pl.program_id(0) == slot // step)(
                functools.partial(store, chunk_ref, i, values[slot % step])
            )
            slot += 1


def polar_call(start, first, count, step, carried, chunks):
    shape = start.shape[1:]
    base = first // step
    block = pl.BlockSpec((step,) + shape, lambda g: (base + g, 0, 0, 0))
    return pl.pallas_call(
        functools.partial(polar_kernel, carried=len(carried), chunks=chunks),
        grid=(count // step,),
        in_specs=[block] + [pl.BlockSpec(memory_space=pl.ANY)] * len(carried),
        out_specs=[block, pl.BlockSpec((step,) + shape, lambda g: (g, 0, 0, 0))]
        + [pl.BlockSpec((size,) + shape, lambda g: (0, 0, 0, 0)) for size in chunks],
        out_shape=[jax.ShapeDtypeStruct((size,) + shape, start.dtype) for size in (start.shape[0], count, *chunks)],
        input_output_aliases={1: 0} if carried else {},
        compiler_params=pltpu.CompilerParams(vmem_limit_bytes=VMEM),
        name="polar",
    )(pltpu.with_memory_space_constraint(start, pltpu.HBM), *carried)


def take_kernel(start_ref, out_ref, sem):
    copy = pltpu.make_async_copy(start_ref.at[pl.ds(0, out_ref.shape[0])], out_ref, sem)
    copy.start()
    copy.wait()


def take_call(start, size):
    return pl.pallas_call(
        take_kernel,
        in_specs=[pl.BlockSpec(memory_space=pltpu.HBM)],
        out_specs=pl.BlockSpec(memory_space=pltpu.VMEM),
        out_shape=jax.ShapeDtypeStruct((size,) + start.shape[1:], start.dtype),
        scratch_shapes=[pltpu.SemaphoreType.DMA],
        compiler_params=pltpu.CompilerParams(vmem_limit_bytes=VMEM),
        name="take",
    )(pltpu.with_memory_space_constraint(start, pltpu.HBM))


def sandwich_kernel(rotation_ref, correlation_ref, *out_refs):
    for i in range(rotation_ref.shape[0]):
        left = split(jnp.concatenate([rotation_ref[i, 0].T, rotation_ref[i, 1].T], 1))
        for d in range(2):
            right = split(jnp.concatenate([correlation_ref[i, d, 0], correlation_ref[i, d, 1]], 1))
            out_refs[d][i] = product(left, both(adjoint_right_form, right))


def sandwich_call(rotation, correlations, step):
    count, _, n, _ = rotation.shape
    return pl.pallas_call(
        sandwich_kernel,
        grid=(count // step,),
        in_specs=[
            pl.BlockSpec((step, 2, n, n), lambda g: (g, 0, 0, 0)),
            pl.BlockSpec((step, 2, 2, n, n), lambda g: (g, 0, 0, 0, 0)),
        ],
        out_specs=[pl.BlockSpec((step, n, 2 * n), lambda g: (g, 0, 0))] * 2,
        out_shape=[jax.ShapeDtypeStruct((count, n, 2 * n), jnp.float32)] * 2,
        compiler_params=pltpu.CompilerParams(vmem_limit_bytes=VMEM),
        name="sandwich",
    )(rotation, correlations)


def column_terms(rotated):
    n = rotated.shape[0]
    unit = identity(n)
    real = jnp.sum(rotated[:, :n] * unit, axis=0, keepdims=True)
    imag = jnp.sum(rotated[:, n:] * unit, axis=0, keepdims=True)
    phase = jnp.arctan2(imag, real)
    modulus = real * real + imag * imag
    w_real = imag / modulus
    w_imag = real / modulus
    return phase, (real + phase * w_real, phase * w_imag - imag, w_real, w_imag)


def store_rows(rows_ref, i, rows):
    for r, row in enumerate(rows):
        rows_ref[i, r : r + 1] = row


def load_rows(rows_ref, i):
    return [rows_ref[i, r : r + 1] for r in range(4)]


def scaled(matrix, v_real, v_imag):
    n = matrix.shape[0]
    real, imag = matrix[:, :n], matrix[:, n:]
    return real * v_real - imag * v_imag, real * v_imag + imag * v_real


def combine(parts_ref, k, matrices, rows):
    real, imag = (
        sum(pair) for pair in zip(*(scaled(m, 2.0 * r[0], 2.0 * r[1]) for m, r in zip(matrices, rows)))
    )
    parts_ref[k, 0] = real - real.T
    parts_ref[k, 1] = imag + imag.T
    for d in range(2):
        real, imag = scaled(matrices[d], 2.0 * rows[d][2], 2.0 * rows[d][3])
        parts_ref[k, 2 + 4 * d] = real
        parts_ref[k, 3 + 4 * d] = imag
        parts_ref[k, 4 + 4 * d] = real.T
        parts_ref[k, 5 + 4 * d] = imag.T


def slab_kernel(
    order_ref, slots_ref, before_ref, plane_ref, plane_rows, sandwich_ref, own_ref, *refs, pieces
):
    piece_refs, (out_ref, rows_ref, parts_ref, total_ref, received_ref) = refs[:pieces], refs[pieces:]
    count, _, n, _ = own_ref.shape
    first = 0
    for piece_ref in piece_refs:
        received_ref[first : first + piece_ref.shape[0]] = piece_ref[...]
        first += piece_ref.shape[0]

    def group(g, total):
        rotated = []
        for i in range(GROUP):
            slot = slots_ref[g * GROUP + i]
            local = slot % count
            remote = slot >= count
            partner = [jnp.where(remote, received_ref[local, p], own_ref[local, p]) for p in range(2)]
            right = both(right_form, split(jnp.concatenate(partner, 1)))
            rotated.append(product(split(sandwich_ref[g * GROUP + i]), right))
        for i, matrix in enumerate(rotated):
            out_ref[g * GROUP + i] = matrix
            phase, rows = column_terms(matrix)
            store_rows(rows_ref, g * GROUP + i, rows)
            total = total + phase
        return total

    total_ref[...] = before_ref[...]
    total_ref[1:2] = lax.fori_loop(0, count // GROUP, group, jnp.zeros((1, n), jnp.float32))

    @pl.loop(0, plane_ref.shape[0])
    def _(slot):
        k = order_ref[slot]
        combine(
            parts_ref,
            k,
            (plane_ref[slot], out_ref[k]),
            (load_rows(plane_rows, slot), load_rows(rows_ref, k)),
        )


def slab_call(order, slots, total, plane, plane_rows, sandwich, own, pieces):
    count, n, _ = sandwich.shape
    whole = pl.BlockSpec(memory_space=pltpu.VMEM)
    scalars = pl.BlockSpec(memory_space=pltpu.SMEM)
    return pl.pallas_call(
        functools.partial(slab_kernel, pieces=len(pieces)),
        in_specs=[scalars] * 2 + [whole] * (5 + len(pieces)),
        out_specs=[whole] * 4,
        out_shape=[
            jax.ShapeDtypeStruct((count, n, 2 * n), jnp.float32),
            jax.ShapeDtypeStruct((count, 8, n), jnp.float32),
            jax.ShapeDtypeStruct((count, 10, n, n), jnp.float32),
            jax.ShapeDtypeStruct((2, n), jnp.float32),
        ],
        scratch_shapes=[pltpu.VMEM(own.shape, own.dtype)],
        compiler_params=pltpu.CompilerParams(vmem_limit_bytes=VMEM),
        name="slab",
    )(order, slots, total, plane, plane_rows, sandwich, own, *pieces)


def plane_products(partner_ref, picked, raw, finish):
    count = partner_ref.shape[0]
    total = jnp.zeros((1, partner_ref.shape[-1]), jnp.float32)
    for begin in range(0, count, GROUP):
        group = range(begin, min(begin + GROUP, count))
        pairs = [(partner_ref[i, 0], partner_ref[i, 1]) for i in group]
        partners = polar(pairs) if raw else [jnp.concatenate(pair, 1) for pair in pairs]
        rotated = [
            product(split(picked(i)), both(right_form, split(partner))) for i, partner in zip(group, partners)
        ]
        for i, matrix in zip(group, rotated):
            phase, rows = column_terms(matrix)
            finish(i, matrix, rows)
            total = total + phase
    return total


def plane_kernel(order_ref, sandwich_ref, partner_ref, before_ref, out_ref, rows_ref, total_ref, *, first):
    def finish(i, matrix, rows):
        out_ref[first + i] = matrix
        store_rows(rows_ref, first + i, rows)

    total = plane_products(partner_ref, lambda i: sandwich_ref[order_ref[first + i]], True, finish)
    total_ref[...] = before_ref[...]
    total_ref[0:1] = total_ref[0:1] + total


def plane_call(order, sandwich, partner, first, total):
    size, _, n, _ = partner.shape
    whole = pl.BlockSpec(memory_space=pltpu.VMEM)
    return pl.pallas_call(
        functools.partial(plane_kernel, first=first),
        in_specs=[pl.BlockSpec(memory_space=pltpu.SMEM)] + [whole] * 3,
        out_specs=[whole] * 3,
        out_shape=[
            jax.ShapeDtypeStruct((size, n, 2 * n), jnp.float32),
            jax.ShapeDtypeStruct((size, 8, n), jnp.float32),
            jax.ShapeDtypeStruct((2, n), jnp.float32),
        ],
        compiler_params=pltpu.CompilerParams(vmem_limit_bytes=VMEM),
        name="plane",
    )(order, sandwich, partner, total)


def middle_kernel(
    order_ref, sandwich_ref, partner_ref, before_ref, slab_ref, slab_rows, _, parts_ref, total_ref, last_ref, *, first
):
    size = partner_ref.shape[0]
    for i in range(last_ref.shape[0]):
        last_ref[i] = sandwich_ref[order_ref[first + size + i]]

    def finish(i, matrix, rows):
        k = order_ref[first + i]
        combine(parts_ref, k, (matrix, slab_ref[k]), (rows, load_rows(slab_rows, k)))

    total = plane_products(partner_ref, lambda i: sandwich_ref[order_ref[first + i]], False, finish)
    total_ref[...] = before_ref[...]
    total_ref[0:1] = total_ref[0:1] + total


def middle_call(order, sandwich, partner, first, total, slab, slab_rows, parts, last):
    _, n, width = sandwich.shape
    whole = pl.BlockSpec(memory_space=pltpu.VMEM)
    return pl.pallas_call(
        functools.partial(middle_kernel, first=first),
        in_specs=[pl.BlockSpec(memory_space=pltpu.SMEM)] + [whole] * 6,
        out_specs=[whole] * 3,
        out_shape=[
            jax.ShapeDtypeStruct(parts.shape, parts.dtype),
            jax.ShapeDtypeStruct(total.shape, total.dtype),
            jax.ShapeDtypeStruct((last, n, width), sandwich.dtype),
        ],
        input_output_aliases={6: 0},
        compiler_params=pltpu.CompilerParams(vmem_limit_bytes=VMEM),
        name="middle",
    )(order, sandwich, partner, total, slab, slab_rows, parts)


def last_kernel(sandwich_ref, partner_ref, before_ref, out_ref, rows_ref, total_ref):
    def finish(i, matrix, rows):
        out_ref[i] = matrix
        store_rows(rows_ref, i, rows)

    total = plane_products(partner_ref, lambda i: sandwich_ref[i], False, finish)
    total_ref[...] = before_ref[...]
    total_ref[0:1] = total_ref[0:1] + total


def last_call(sandwich, partner, total):
    size, n, width = sandwich.shape
    whole = pl.BlockSpec(memory_space=pltpu.VMEM)
    return pl.pallas_call(
        last_kernel,
        in_specs=[whole] * 3,
        out_specs=[whole] * 3,
        out_shape=[
            jax.ShapeDtypeStruct((size, n, width), jnp.float32),
            jax.ShapeDtypeStruct((size, 8, n), jnp.float32),
            jax.ShapeDtypeStruct(total.shape, total.dtype),
        ],
        compiler_params=pltpu.CompilerParams(vmem_limit_bytes=VMEM),
        name="last",
    )(sandwich, partner, total)


def combine_kernel(order_ref, plane_ref, plane_rows, slab_ref, slab_rows, _, parts_ref, *, first):
    for i in range(plane_ref.shape[0]):
        k = order_ref[first + i]
        combine(
            parts_ref, k, (plane_ref[i], slab_ref[k]), (load_rows(plane_rows, i), load_rows(slab_rows, k))
        )


def combine_call(order, plane, plane_rows, slab, slab_rows, parts, first):
    whole = pl.BlockSpec(memory_space=pltpu.VMEM)
    return pl.pallas_call(
        functools.partial(combine_kernel, first=first),
        in_specs=[pl.BlockSpec(memory_space=pltpu.SMEM)] + [whole] * 5,
        out_specs=whole,
        out_shape=jax.ShapeDtypeStruct(parts.shape, parts.dtype),
        input_output_aliases={5: 0},
        compiler_params=pltpu.CompilerParams(vmem_limit_bytes=VMEM),
        name="combine",
    )(order, plane, plane_rows, slab, slab_rows, parts)


def gradient_kernel(first_ref, second_ref, parts_ref, out_ref, centres_ref, buffer, small, sems, small_sem, *, everything):
    count, _, n, _ = buffer.shape
    centres = (first_ref[...] + second_ref[...]) / (-2.0 * everything)
    small[...] = centres
    small_copy = pltpu.make_async_copy(small, centres_ref, small_sem)
    small_copy.start()
    across = [centres[d : d + 1] for d in range(2)]
    down = [jnp.broadcast_to(row, (n, n)).T for row in across]

    def copy_out(k):
        return pltpu.make_async_copy(buffer.at[k], out_ref.at[k], sems.at[k])

    @pl.loop(0, count)
    def _(k):
        real, imag = parts_ref[k, 0], parts_ref[k, 1]
        for d in range(2):
            real = real + (parts_ref[k, 2 + 4 * d] * across[d] - parts_ref[k, 4 + 4 * d] * down[d])
            imag = imag + (parts_ref[k, 3 + 4 * d] * across[d] + parts_ref[k, 5 + 4 * d] * down[d])
        for p, half in enumerate((real, imag)):
            buffer[k, p] = half
            pltpu.make_async_copy(buffer.at[k, p], out_ref.at[k, p], sems.at[k]).start()

    small_copy.wait()

    @pl.loop(0, count)
    def _(k):
        copy_out(k).wait()


def gradient_call(totals, parts, everything):
    count, _, n, _ = parts.shape
    whole = pl.BlockSpec(memory_space=pltpu.VMEM)
    return pl.pallas_call(
        functools.partial(gradient_kernel, everything=everything),
        in_specs=[whole] * 3,
        out_specs=[pl.BlockSpec(memory_space=pl.ANY)] * 2,
        out_shape=[
            jax.ShapeDtypeStruct((count, 2, n, n), jnp.float32),
            jax.ShapeDtypeStruct((2, n), jnp.float32),
        ],
        scratch_shapes=[
            pltpu.VMEM((count, 2, n, n), jnp.float32),
            pltpu.VMEM((2, n), jnp.float32),
            pltpu.SemaphoreType.DMA((count,)),
            pltpu.SemaphoreType.DMA,
        ],
        compiler_params=pltpu.CompilerParams(vmem_limit_bytes=VMEM),
        name="gradient",
    )(*totals, parts)


def shifted(value, axis, steps):
    count = lax.axis_size(axis)
    return lax.ppermute(value, axis, [(source, (source + steps) % count) for source in range(count)])


def reduce_parts(value):
    count = lax.axis_size("kxy")
    if lax.axis_size("kz") != 2 or count & (count - 1) or count < 4:
        return lax.psum(value, ("kxy", "kz")), jnp.zeros_like(value)

    def swapped(value, bits, core):
        pairs = [(2 * s + c, 2 * (s ^ bits) + (c ^ core)) for s in range(count) for c in range(2)]
        return lax.ppermute(value, ("kxy", "kz"), pairs)

    value = value + swapped(value, 0, 1) + (swapped(value, 1, 0) + swapped(value, 1, 1))
    distance = count // 2
    while distance > 2:
        value = value + swapped(value, distance, 1)
        distance //= 2
    return value, swapped(value, distance, 1)


def body(start_rotation, correlations, neighbours):
    count = start_rotation.shape[0]
    block_index = lax.axis_index("kxy") * lax.axis_size("kz") + lax.axis_index("kz")
    everything = count * lax.axis_size("kxy") * lax.axis_size("kz")
    plane_slots = neighbours[:, 0] % count
    positions = jnp.arange(count, dtype=jnp.int32)
    order = jnp.max(jnp.where(plane_slots[:, None] == positions[None], positions[:, None], 0), axis=0)
    remote = (neighbours[:, 1] // count != block_index).astype(jnp.int32)
    slab_slots = neighbours[:, 1] % count + count * remote

    partners = [shifted(take_call(start_rotation, RAW), "kxy", -2)]
    rotation, late, *parts = polar_call(start_rotation, RAW, count - RAW, GROUP, [], CHUNKS)
    partners += [shifted(part, "kxy", -2) for part in parts]
    rotation, early = polar_call(start_rotation, 0, RAW, GROUP, [rotation], ())
    from_slab = [shifted(part, "kz", -1) for part in (early, late)]
    for_plane, for_slab = sandwich_call(rotation, correlations, GROUP)
    total = jnp.zeros((2, rotation.shape[-1]), jnp.float32)
    plane, plane_rows, total = plane_call(order, for_plane, partners[0], 0, total)
    slab, slab_rows, parts, total = slab_call(
        order, slab_slots, total, plane, plane_rows, for_slab, rotation, from_slab
    )
    parts, total, for_last = middle_call(
        order, for_plane, partners[1], RAW, total, slab, slab_rows, parts, CHUNKS[-1]
    )
    plane, plane_rows, total = last_call(for_last, partners[2], total)
    totals = reduce_parts(total)
    parts = combine_call(order, plane, plane_rows, slab, slab_rows, parts, count - CHUNKS[-1])
    gradient, centres = gradient_call(totals, parts, everything)
    return (rotation, gradient, centres)


def solution(mesh):
    in_specs = (
        P(("grp", "kxy", "kz"), None, None, None),
        P(("grp", "kxy", "kz"), None, None, None, None),
        P(("grp", "kxy", "kz"), None),
    )
    out_specs = (
        P(("grp", "kxy", "kz"), None, None, None),
        P(("grp", "kxy", "kz"), None, None, None),
        P("grp", None),
    )
    return jax.shard_map(body, mesh=mesh, in_specs=in_specs, out_specs=out_specs, check_vma=False)
```

```python
import functools

import jax
import jax.numpy as jnp
from jax import lax
from jax.experimental import pallas as pl
from jax.experimental.pallas import tpu as pltpu
from jax.sharding import PartitionSpec as P

NS_STEPS = 3
RAW = 8
CHUNKS = (6, 2)
GROUP = 4
VMEM = 16 << 20


def dot(left, right, contract):
    return lax.dot_general(left, right, ((contract), ((), ())), preferred_element_type=jnp.float32)


def split(value):
    high = value.astype(jnp.bfloat16)
    return high, (value - high.astype(jnp.float32)).astype(jnp.bfloat16)


def product(left, right, contract=((1,), (0,))):
    return dot(left[0], right[0], contract) + (
        dot(left[0], right[1], contract) + dot(left[1], right[0], contract)
    )


def both(function, pair):
    return tuple(function(half) for half in pair)


def right_form(half):
    n = half.shape[0]
    return jnp.concatenate([half, jnp.concatenate([-half[:, n:], half[:, :n]], 1)], 0)


def adjoint_right_form(half):
    n = half.shape[0]
    return jnp.concatenate([half, jnp.concatenate([half[:, n:], -half[:, :n]], 1)], 0)


def identity(n):
    rows = lax.broadcasted_iota(jnp.int32, (n, n), 0)
    return (rows == lax.broadcasted_iota(jnp.int32, (n, n), 1)).astype(jnp.float32)


def polar(pairs):
    n = pairs[0][0].shape[0]
    unit = identity(n)
    unit = jnp.concatenate([1.5 * unit, jnp.zeros_like(unit)], 1)
    current = []
    for real, imag in pairs:
        scale = 1.0 / jnp.sqrt(jnp.sum(real * real + imag * imag) / n + 1e-06)
        current.append(jnp.concatenate([real * scale, imag * scale], 1))
    for _ in range(NS_STEPS):
        left = [split(value) for value in current]
        right = [both(right_form, pair) for pair in left]
        gram = [product(a, b, ((1,), (1,))) for a, b in zip(left, right)]
        factor = [split(unit - 0.5 * value) for value in gram]
        current = [product(a, b) for a, b in zip(factor, right)]
    return current


def polar_kernel(start_ref, *refs, carried, chunks):
    out_refs, chunk_refs = refs[carried : carried + 2], refs[carried + 2 :]
    n = start_ref.shape[-1]
    step = start_ref.shape[0]
    values = polar([(start_ref[i, 0], start_ref[i, 1]) for i in range(step)])

    def store(ref, i, value):
        ref[i, 0] = value[:, :n]
        ref[i, 1] = value[:, n:]

    for i, value in enumerate(values):
        for out_ref in out_refs:
            store(out_ref, i, value)
    slot = 0
    for chunk_ref, size in zip(chunk_refs, chunks):
        for i in range(size):
            pl.when(pl.program_id(0) == slot // step)(
                functools.partial(store, chunk_ref, i, values[slot % step])
            )
            slot += 1


def polar_call(start, first, count, step, carried, chunks):
    shape = start.shape[1:]
    base = first // step
    block = pl.BlockSpec((step,) + shape, lambda g: (base + g, 0, 0, 0))
    return pl.pallas_call(
        functools.partial(polar_kernel, carried=len(carried), chunks=chunks),
        grid=(count // step,),
        in_specs=[block] + [pl.BlockSpec(memory_space=pl.ANY)] * len(carried),
        out_specs=[block, pl.BlockSpec((step,) + shape, lambda g: (g, 0, 0, 0))]
        + [pl.BlockSpec((size,) + shape, lambda g: (0, 0, 0, 0)) for size in chunks],
        out_shape=[jax.ShapeDtypeStruct((size,) + shape, start.dtype) for size in (start.shape[0], count, *chunks)],
        input_output_aliases={1: 0} if carried else {},
        compiler_params=pltpu.CompilerParams(vmem_limit_bytes=VMEM),
        name="polar",
    )(pltpu.with_memory_space_constraint(start, pltpu.HBM), *carried)


def take_kernel(start_ref, out_ref, sem):
    copy = pltpu.make_async_copy(start_ref.at[pl.ds(0, out_ref.shape[0])], out_ref, sem)
    copy.start()
    copy.wait()


def take_call(start, size):
    return pl.pallas_call(
        take_kernel,
        in_specs=[pl.BlockSpec(memory_space=pltpu.HBM)],
        out_specs=pl.BlockSpec(memory_space=pltpu.VMEM),
        out_shape=jax.ShapeDtypeStruct((size,) + start.shape[1:], start.dtype),
        scratch_shapes=[pltpu.SemaphoreType.DMA],
        compiler_params=pltpu.CompilerParams(vmem_limit_bytes=VMEM),
        name="take",
    )(pltpu.with_memory_space_constraint(start, pltpu.HBM))


def sandwich_kernel(rotation_ref, correlation_ref, *out_refs):
    for i in range(rotation_ref.shape[0]):
        left = split(jnp.concatenate([rotation_ref[i, 0].T, rotation_ref[i, 1].T], 1))
        for d in range(2):
            right = split(jnp.concatenate([correlation_ref[i, d, 0], correlation_ref[i, d, 1]], 1))
            out_refs[d][i] = product(left, both(adjoint_right_form, right))


def sandwich_call(rotation, correlations, step):
    count, _, n, _ = rotation.shape
    return pl.pallas_call(
        sandwich_kernel,
        grid=(count // step,),
        in_specs=[
            pl.BlockSpec((step, 2, n, n), lambda g: (g, 0, 0, 0)),
            pl.BlockSpec((step, 2, 2, n, n), lambda g: (g, 0, 0, 0, 0)),
        ],
        out_specs=[pl.BlockSpec((step, n, 2 * n), lambda g: (g, 0, 0))] * 2,
        out_shape=[jax.ShapeDtypeStruct((count, n, 2 * n), jnp.float32)] * 2,
        compiler_params=pltpu.CompilerParams(vmem_limit_bytes=VMEM),
        name="sandwich",
    )(rotation, correlations)


def column_terms(rotated):
    n = rotated.shape[0]
    unit = identity(n)
    real = jnp.sum(rotated[:, :n] * unit, axis=0, keepdims=True)
    imag = jnp.sum(rotated[:, n:] * unit, axis=0, keepdims=True)
    phase = jnp.arctan2(imag, real)
    modulus = real * real + imag * imag
    w_real = imag / modulus
    w_imag = real / modulus
    return phase, (real + phase * w_real, phase * w_imag - imag, w_real, w_imag)


def store_rows(rows_ref, i, rows):
    for r, row in enumerate(rows):
        rows_ref[i, r : r + 1] = row


def load_rows(rows_ref, i):
    return [rows_ref[i, r : r + 1] for r in range(4)]


def scaled(matrix, v_real, v_imag):
    n = matrix.shape[0]
    real, imag = matrix[:, :n], matrix[:, n:]
    return real * v_real - imag * v_imag, real * v_imag + imag * v_real


def combine(parts_ref, k, matrices, rows):
    real, imag = (
        sum(pair) for pair in zip(*(scaled(m, 2.0 * r[0], 2.0 * r[1]) for m, r in zip(matrices, rows)))
    )
    parts_ref[k, 0] = real - real.T
    parts_ref[k, 1] = imag + imag.T
    for d in range(2):
        real, imag = scaled(matrices[d], 2.0 * rows[d][2], 2.0 * rows[d][3])
        parts_ref[k, 2 + 4 * d] = real
        parts_ref[k, 3 + 4 * d] = imag
        parts_ref[k, 4 + 4 * d] = real.T
        parts_ref[k, 5 + 4 * d] = imag.T


def slab_kernel(
    order_ref, slots_ref, before_ref, plane_ref, plane_rows, sandwich_ref, own_ref, *refs, pieces
):
    piece_refs, (out_ref, rows_ref, parts_ref, total_ref, received_ref) = refs[:pieces], refs[pieces:]
    count, _, n, _ = own_ref.shape
    first = 0
    for piece_ref in piece_refs:
        received_ref[first : first + piece_ref.shape[0]] = piece_ref[...]
        first += piece_ref.shape[0]

    def group(g, total):
        rotated = []
        for i in range(GROUP):
            slot = slots_ref[g * GROUP + i]
            local = slot % count
            remote = slot >= count
            partner = [jnp.where(remote, received_ref[local, p], own_ref[local, p]) for p in range(2)]
            right = both(right_form, split(jnp.concatenate(partner, 1)))
            rotated.append(product(split(sandwich_ref[g * GROUP + i]), right))
        for i, matrix in enumerate(rotated):
            out_ref[g * GROUP + i] = matrix
            phase, rows = column_terms(matrix)
            store_rows(rows_ref, g * GROUP + i, rows)
            total = total + phase
        return total

    total_ref[...] = before_ref[...]
    total_ref[1:2] = lax.fori_loop(0, count // GROUP, group, jnp.zeros((1, n), jnp.float32))

    @pl.loop(0, plane_ref.shape[0])
    def _(slot):
        k = order_ref[slot]
        combine(
            parts_ref,
            k,
            (plane_ref[slot], out_ref[k]),
            (load_rows(plane_rows, slot), load_rows(rows_ref, k)),
        )


def slab_call(order, slots, total, plane, plane_rows, sandwich, own, pieces):
    count, n, _ = sandwich.shape
    whole = pl.BlockSpec(memory_space=pltpu.VMEM)
    scalars = pl.BlockSpec(memory_space=pltpu.SMEM)
    return pl.pallas_call(
        functools.partial(slab_kernel, pieces=len(pieces)),
        in_specs=[scalars] * 2 + [whole] * (5 + len(pieces)),
        out_specs=[whole] * 4,
        out_shape=[
            jax.ShapeDtypeStruct((count, n, 2 * n), jnp.float32),
            jax.ShapeDtypeStruct((count, 8, n), jnp.float32),
            jax.ShapeDtypeStruct((count, 10, n, n), jnp.float32),
            jax.ShapeDtypeStruct((2, n), jnp.float32),
        ],
        scratch_shapes=[pltpu.VMEM(own.shape, own.dtype)],
        compiler_params=pltpu.CompilerParams(vmem_limit_bytes=VMEM),
        name="slab",
    )(order, slots, total, plane, plane_rows, sandwich, own, *pieces)


def plane_products(partner_ref, picked, raw, finish):
    count = partner_ref.shape[0]
    total = jnp.zeros((1, partner_ref.shape[-1]), jnp.float32)
    for begin in range(0, count, GROUP):
        group = range(begin, min(begin + GROUP, count))
        pairs = [(partner_ref[i, 0], partner_ref[i, 1]) for i in group]
        partners = polar(pairs) if raw else [jnp.concatenate(pair, 1) for pair in pairs]
        rotated = [
            product(split(picked(i)), both(right_form, split(partner))) for i, partner in zip(group, partners)
        ]
        for i, matrix in zip(group, rotated):
            phase, rows = column_terms(matrix)
            finish(i, matrix, rows)
            total = total + phase
    return total


def plane_kernel(order_ref, sandwich_ref, partner_ref, before_ref, out_ref, rows_ref, total_ref, *, first):
    def finish(i, matrix, rows):
        out_ref[first + i] = matrix
        store_rows(rows_ref, first + i, rows)

    total = plane_products(partner_ref, lambda i: sandwich_ref[order_ref[first + i]], True, finish)
    total_ref[...] = before_ref[...]
    total_ref[0:1] = total_ref[0:1] + total


def plane_call(order, sandwich, partner, first, total):
    size, _, n, _ = partner.shape
    whole = pl.BlockSpec(memory_space=pltpu.VMEM)
    return pl.pallas_call(
        functools.partial(plane_kernel, first=first),
        in_specs=[pl.BlockSpec(memory_space=pltpu.SMEM)] + [whole] * 3,
        out_specs=[whole] * 3,
        out_shape=[
            jax.ShapeDtypeStruct((size, n, 2 * n), jnp.float32),
            jax.ShapeDtypeStruct((size, 8, n), jnp.float32),
            jax.ShapeDtypeStruct((2, n), jnp.float32),
        ],
        compiler_params=pltpu.CompilerParams(vmem_limit_bytes=VMEM),
        name="plane",
    )(order, sandwich, partner, total)


def middle_kernel(
    order_ref, sandwich_ref, partner_ref, before_ref, slab_ref, slab_rows, _, parts_ref, total_ref, last_ref, *, first
):
    size = partner_ref.shape[0]
    for i in range(last_ref.shape[0]):
        last_ref[i] = sandwich_ref[order_ref[first + size + i]]

    def finish(i, matrix, rows):
        k = order_ref[first + i]
        combine(parts_ref, k, (matrix, slab_ref[k]), (rows, load_rows(slab_rows, k)))

    total = plane_products(partner_ref, lambda i: sandwich_ref[order_ref[first + i]], False, finish)
    total_ref[...] = before_ref[...]
    total_ref[0:1] = total_ref[0:1] + total


def middle_call(order, sandwich, partner, first, total, slab, slab_rows, parts, last):
    _, n, width = sandwich.shape
    whole = pl.BlockSpec(memory_space=pltpu.VMEM)
    return pl.pallas_call(
        functools.partial(middle_kernel, first=first),
        in_specs=[pl.BlockSpec(memory_space=pltpu.SMEM)] + [whole] * 6,
        out_specs=[whole] * 3,
        out_shape=[
            jax.ShapeDtypeStruct(parts.shape, parts.dtype),
            jax.ShapeDtypeStruct(total.shape, total.dtype),
            jax.ShapeDtypeStruct((last, n, width), sandwich.dtype),
        ],
        input_output_aliases={6: 0},
        compiler_params=pltpu.CompilerParams(vmem_limit_bytes=VMEM),
        name="middle",
    )(order, sandwich, partner, total, slab, slab_rows, parts)


def last_kernel(sandwich_ref, partner_ref, before_ref, out_ref, rows_ref, total_ref):
    def finish(i, matrix, rows):
        out_ref[i] = matrix
        store_rows(rows_ref, i, rows)

    total = plane_products(partner_ref, lambda i: sandwich_ref[i], False, finish)
    total_ref[...] = before_ref[...]
    total_ref[0:1] = total_ref[0:1] + total


def last_call(sandwich, partner, total):
    size, n, width = sandwich.shape
    whole = pl.BlockSpec(memory_space=pltpu.VMEM)
    return pl.pallas_call(
        last_kernel,
        in_specs=[whole] * 3,
        out_specs=[whole] * 3,
        out_shape=[
            jax.ShapeDtypeStruct((size, n, width), jnp.float32),
            jax.ShapeDtypeStruct((size, 8, n), jnp.float32),
            jax.ShapeDtypeStruct(total.shape, total.dtype),
        ],
        compiler_params=pltpu.CompilerParams(vmem_limit_bytes=VMEM),
        name="last",
    )(sandwich, partner, total)


def combine_kernel(order_ref, plane_ref, plane_rows, slab_ref, slab_rows, _, parts_ref, *, first):
    for i in range(plane_ref.shape[0]):
        k = order_ref[first + i]
        combine(
            parts_ref, k, (plane_ref[i], slab_ref[k]), (load_rows(plane_rows, i), load_rows(slab_rows, k))
        )


def combine_call(order, plane, plane_rows, slab, slab_rows, parts, first):
    whole = pl.BlockSpec(memory_space=pltpu.VMEM)
    return pl.pallas_call(
        functools.partial(combine_kernel, first=first),
        in_specs=[pl.BlockSpec(memory_space=pltpu.SMEM)] + [whole] * 5,
        out_specs=whole,
        out_shape=jax.ShapeDtypeStruct(parts.shape, parts.dtype),
        input_output_aliases={5: 0},
        compiler_params=pltpu.CompilerParams(vmem_limit_bytes=VMEM),
        name="combine",
    )(order, plane, plane_rows, slab, slab_rows, parts)


def gradient_kernel(first_ref, second_ref, parts_ref, out_ref, centres_ref, buffer, small, sems, small_sem, *, everything):
    count, _, n, _ = buffer.shape
    centres = (first_ref[...] + second_ref[...]) / (-2.0 * everything)
    small[...] = centres
    small_copy = pltpu.make_async_copy(small, centres_ref, small_sem)
    small_copy.start()
    across = [centres[d : d + 1] for d in range(2)]
    down = [jnp.broadcast_to(row, (n, n)).T for row in across]

    def copy_out(k):
        return pltpu.make_async_copy(buffer.at[k], out_ref.at[k], sems.at[k])

    @pl.loop(0, count)
    def _(k):
        real, imag = parts_ref[k, 0], parts_ref[k, 1]
        for d in range(2):
            real = real + (parts_ref[k, 2 + 4 * d] * across[d] - parts_ref[k, 4 + 4 * d] * down[d])
            imag = imag + (parts_ref[k, 3 + 4 * d] * across[d] + parts_ref[k, 5 + 4 * d] * down[d])
        for p, half in enumerate((real, imag)):
            buffer[k, p] = half
            pltpu.make_async_copy(buffer.at[k, p], out_ref.at[k, p], sems.at[k]).start()

    small_copy.wait()

    @pl.loop(0, count)
    def _(k):
        copy_out(k).wait()


def gradient_call(totals, parts, everything):
    count, _, n, _ = parts.shape
    whole = pl.BlockSpec(memory_space=pltpu.VMEM)
    return pl.pallas_call(
        functools.partial(gradient_kernel, everything=everything),
        in_specs=[whole] * 3,
        out_specs=[pl.BlockSpec(memory_space=pl.ANY)] * 2,
        out_shape=[
            jax.ShapeDtypeStruct((count, 2, n, n), jnp.float32),
            jax.ShapeDtypeStruct((2, n), jnp.float32),
        ],
        scratch_shapes=[
            pltpu.VMEM((count, 2, n, n), jnp.float32),
            pltpu.VMEM((2, n), jnp.float32),
            pltpu.SemaphoreType.DMA((count,)),
            pltpu.SemaphoreType.DMA,
        ],
        compiler_params=pltpu.CompilerParams(vmem_limit_bytes=VMEM),
        name="gradient",
    )(*totals, parts)


def shifted(value, axis, steps):
    count = lax.axis_size(axis)
    return lax.ppermute(value, axis, [(source, (source + steps) % count) for source in range(count)])


def reduce_parts(value):
    count = lax.axis_size("kxy")
    if lax.axis_size("kz") != 2 or count & (count - 1) or count < 4:
        return lax.psum(value, ("kxy", "kz")), jnp.zeros_like(value)

    def swapped(value, bits, core):
        pairs = [(2 * s + c, 2 * (s ^ bits) + (c ^ core)) for s in range(count) for c in range(2)]
        return lax.ppermute(value, ("kxy", "kz"), pairs)

    value = value + swapped(value, 0, 1) + (swapped(value, 1, 0) + swapped(value, 1, 1))
    distance = 2
    while 2 * distance < count:
        value = value + swapped(value, distance, 1)
        distance *= 2
    return value, swapped(value, distance, 1)


def body(start_rotation, correlations, neighbours):
    count = start_rotation.shape[0]
    block_index = lax.axis_index("kxy") * lax.axis_size("kz") + lax.axis_index("kz")
    everything = count * lax.axis_size("kxy") * lax.axis_size("kz")
    plane_slots = neighbours[:, 0] % count
    positions = jnp.arange(count, dtype=jnp.int32)
    order = jnp.max(jnp.where(plane_slots[:, None] == positions[None], positions[:, None], 0), axis=0)
    remote = (neighbours[:, 1] // count != block_index).astype(jnp.int32)
    slab_slots = neighbours[:, 1] % count + count * remote

    partners = [shifted(take_call(start_rotation, RAW), "kxy", -2)]
    rotation, late, *parts = polar_call(start_rotation, RAW, count - RAW, GROUP, [], CHUNKS)
    partners += [shifted(part, "kxy", -2) for part in parts]
    rotation, early = polar_call(start_rotation, 0, RAW, GROUP, [rotation], ())
    from_slab = [shifted(part, "kz", -1) for part in (early, late)]
    for_plane, for_slab = sandwich_call(rotation, correlations, GROUP)
    total = jnp.zeros((2, rotation.shape[-1]), jnp.float32)
    plane, plane_rows, total = plane_call(order, for_plane, partners[0], 0, total)
    slab, slab_rows, parts, total = slab_call(
        order, slab_slots, total, plane, plane_rows, for_slab, rotation, from_slab
    )
    parts, total, for_last = middle_call(
        order, for_plane, partners[1], RAW, total, slab, slab_rows, parts, CHUNKS[-1]
    )
    plane, plane_rows, total = last_call(for_last, partners[2], total)
    totals = reduce_parts(total)
    parts = combine_call(order, plane, plane_rows, slab, slab_rows, parts, count - CHUNKS[-1])
    gradient, centres = gradient_call(totals, parts, everything)
    return (rotation, gradient, centres)


def solution(mesh):
    in_specs = (
        P(("grp", "kxy", "kz"), None, None, None),
        P(("grp", "kxy", "kz"), None, None, None, None),
        P(("grp", "kxy", "kz"), None),
    )
    out_specs = (
        P(("grp", "kxy", "kz"), None, None, None),
        P(("grp", "kxy", "kz"), None, None, None),
        P("grp", None),
    )
    return jax.shard_map(body, mesh=mesh, in_specs=in_specs, out_specs=out_specs, check_vma=False)
```

```python
import functools

import jax
import jax.numpy as jnp
from jax import lax
from jax.experimental import pallas as pl
from jax.experimental.pallas import tpu as pltpu
from jax.sharding import PartitionSpec as P

NS_STEPS = 3
RAW = 8
CHUNKS = (6, 2)
GROUP = 4
VMEM = 16 << 20


def dot(left, right, contract):
    return lax.dot_general(left, right, ((contract), ((), ())), preferred_element_type=jnp.float32)


def split(value):
    high = value.astype(jnp.bfloat16)
    return high, (value - high.astype(jnp.float32)).astype(jnp.bfloat16)


def product(left, right, contract=((1,), (0,))):
    return dot(left[0], right[0], contract) + (
        dot(left[0], right[1], contract) + dot(left[1], right[0], contract)
    )


def both(function, pair):
    return tuple(function(half) for half in pair)


def right_form(half):
    n = half.shape[0]
    return jnp.concatenate([half, jnp.concatenate([-half[:, n:], half[:, :n]], 1)], 0)


def adjoint_right_form(half):
    n = half.shape[0]
    return jnp.concatenate([half, jnp.concatenate([half[:, n:], -half[:, :n]], 1)], 0)


def identity(n):
    rows = lax.broadcasted_iota(jnp.int32, (n, n), 0)
    return (rows == lax.broadcasted_iota(jnp.int32, (n, n), 1)).astype(jnp.float32)


def polar(pairs):
    n = pairs[0][0].shape[0]
    unit = identity(n)
    unit = jnp.concatenate([1.5 * unit, jnp.zeros_like(unit)], 1)
    current = []
    for real, imag in pairs:
        scale = 1.0 / jnp.sqrt(jnp.sum(real * real + imag * imag) / n + 1e-06)
        current.append(jnp.concatenate([real * scale, imag * scale], 1))
    for _ in range(NS_STEPS):
        left = [split(value) for value in current]
        right = [both(right_form, pair) for pair in left]
        gram = [product(a, b, ((1,), (1,))) for a, b in zip(left, right)]
        factor = [split(unit - 0.5 * value) for value in gram]
        current = [product(a, b) for a, b in zip(factor, right)]
    return current


def polar_kernel(start_ref, *refs, carried, chunks):
    out_refs, chunk_refs = refs[carried : carried + 2], refs[carried + 2 :]
    n = start_ref.shape[-1]
    step = start_ref.shape[0]
    values = polar([(start_ref[i, 0], start_ref[i, 1]) for i in range(step)])

    def store(ref, i, value):
        ref[i, 0] = value[:, :n]
        ref[i, 1] = value[:, n:]

    for i, value in enumerate(values):
        for out_ref in out_refs:
            store(out_ref, i, value)
    slot = 0
    for chunk_ref, size in zip(chunk_refs, chunks):
        for i in range(size):
            pl.when(pl.program_id(0) == slot // step)(
                functools.partial(store, chunk_ref, i, values[slot % step])
            )
            slot += 1


def polar_call(start, first, count, step, carried, chunks):
    shape = start.shape[1:]
    base = first // step
    block = pl.BlockSpec((step,) + shape, lambda g: (base + g, 0, 0, 0))
    return pl.pallas_call(
        functools.partial(polar_kernel, carried=len(carried), chunks=chunks),
        grid=(count // step,),
        in_specs=[block] + [pl.BlockSpec(memory_space=pl.ANY)] * len(carried),
        out_specs=[block, pl.BlockSpec((step,) + shape, lambda g: (g, 0, 0, 0))]
        + [pl.BlockSpec((size,) + shape, lambda g: (0, 0, 0, 0)) for size in chunks],
        out_shape=[jax.ShapeDtypeStruct((size,) + shape, start.dtype) for size in (start.shape[0], count, *chunks)],
        input_output_aliases={1: 0} if carried else {},
        compiler_params=pltpu.CompilerParams(vmem_limit_bytes=VMEM),
        name="polar",
    )(pltpu.with_memory_space_constraint(start, pltpu.HBM), *carried)


def take_kernel(start_ref, out_ref, sem):
    copy = pltpu.make_async_copy(start_ref.at[pl.ds(0, out_ref.shape[0])], out_ref, sem)
    copy.start()
    copy.wait()


def take_call(start, size):
    return pl.pallas_call(
        take_kernel,
        in_specs=[pl.BlockSpec(memory_space=pltpu.HBM)],
        out_specs=pl.BlockSpec(memory_space=pltpu.VMEM),
        out_shape=jax.ShapeDtypeStruct((size,) + start.shape[1:], start.dtype),
        scratch_shapes=[pltpu.SemaphoreType.DMA],
        compiler_params=pltpu.CompilerParams(vmem_limit_bytes=VMEM),
        name="take",
    )(pltpu.with_memory_space_constraint(start, pltpu.HBM))


def sandwich_kernel(rotation_ref, correlation_ref, *out_refs):
    for i in range(rotation_ref.shape[0]):
        left = split(jnp.concatenate([rotation_ref[i, 0].T, rotation_ref[i, 1].T], 1))
        for d in range(2):
            right = split(jnp.concatenate([correlation_ref[i, d, 0], correlation_ref[i, d, 1]], 1))
            out_refs[d][i] = product(left, both(adjoint_right_form, right))


def sandwich_call(rotation, correlations, step):
    count, _, n, _ = rotation.shape
    return pl.pallas_call(
        sandwich_kernel,
        grid=(count // step,),
        in_specs=[
            pl.BlockSpec((step, 2, n, n), lambda g: (g, 0, 0, 0)),
            pl.BlockSpec((step, 2, 2, n, n), lambda g: (g, 0, 0, 0, 0)),
        ],
        out_specs=[pl.BlockSpec((step, n, 2 * n), lambda g: (g, 0, 0))] * 2,
        out_shape=[jax.ShapeDtypeStruct((count, n, 2 * n), jnp.float32)] * 2,
        compiler_params=pltpu.CompilerParams(vmem_limit_bytes=VMEM),
        name="sandwich",
    )(rotation, correlations)


def column_terms(rotated):
    n = rotated.shape[0]
    unit = identity(n)
    real = jnp.sum(rotated[:, :n] * unit, axis=0, keepdims=True)
    imag = jnp.sum(rotated[:, n:] * unit, axis=0, keepdims=True)
    phase = jnp.arctan2(imag, real)
    modulus = real * real + imag * imag
    w_real = imag / modulus
    w_imag = real / modulus
    return phase, (real + phase * w_real, phase * w_imag - imag, w_real, w_imag)


def store_rows(rows_ref, i, rows):
    for r, row in enumerate(rows):
        rows_ref[i, r : r + 1] = row


def load_rows(rows_ref, i):
    return [rows_ref[i, r : r + 1] for r in range(4)]


def scaled(matrix, v_real, v_imag):
    n = matrix.shape[0]
    real, imag = matrix[:, :n], matrix[:, n:]
    return real * v_real - imag * v_imag, real * v_imag + imag * v_real


def combine(parts_ref, k, matrices, rows):
    real, imag = (
        sum(pair) for pair in zip(*(scaled(m, 2.0 * r[0], 2.0 * r[1]) for m, r in zip(matrices, rows)))
    )
    parts_ref[k, 0] = real - real.T
    parts_ref[k, 1] = imag + imag.T
    for d in range(2):
        real, imag = scaled(matrices[d], 2.0 * rows[d][2], 2.0 * rows[d][3])
        parts_ref[k, 2 + 4 * d] = real
        parts_ref[k, 3 + 4 * d] = imag
        parts_ref[k, 4 + 4 * d] = real.T
        parts_ref[k, 5 + 4 * d] = imag.T


def slab_kernel(
    order_ref, slots_ref, before_ref, plane_ref, plane_rows, sandwich_ref, own_ref, *refs, pieces
):
    piece_refs, (out_ref, rows_ref, parts_ref, total_ref, received_ref) = refs[:pieces], refs[pieces:]
    count, _, n, _ = own_ref.shape
    first = 0
    for piece_ref in piece_refs:
        received_ref[first : first + piece_ref.shape[0]] = piece_ref[...]
        first += piece_ref.shape[0]

    def group(g, total):
        rotated = []
        for i in range(GROUP):
            slot = slots_ref[g * GROUP + i]
            local = slot % count
            remote = slot >= count
            partner = [jnp.where(remote, received_ref[local, p], own_ref[local, p]) for p in range(2)]
            right = both(right_form, split(jnp.concatenate(partner, 1)))
            rotated.append(product(split(sandwich_ref[g * GROUP + i]), right))
        for i, matrix in enumerate(rotated):
            out_ref[g * GROUP + i] = matrix
            phase, rows = column_terms(matrix)
            store_rows(rows_ref, g * GROUP + i, rows)
            total = total + phase
        return total

    total_ref[...] = before_ref[...]
    total_ref[1:2] = lax.fori_loop(0, count // GROUP, group, jnp.zeros((1, n), jnp.float32))

    @pl.loop(0, plane_ref.shape[0])
    def _(slot):
        k = order_ref[slot]
        combine(
            parts_ref,
            k,
            (plane_ref[slot], out_ref[k]),
            (load_rows(plane_rows, slot), load_rows(rows_ref, k)),
        )


def slab_call(order, slots, total, plane, plane_rows, sandwich, own, pieces):
    count, n, _ = sandwich.shape
    whole = pl.BlockSpec(memory_space=pltpu.VMEM)
    scalars = pl.BlockSpec(memory_space=pltpu.SMEM)
    return pl.pallas_call(
        functools.partial(slab_kernel, pieces=len(pieces)),
        in_specs=[scalars] * 2 + [whole] * (5 + len(pieces)),
        out_specs=[whole] * 4,
        out_shape=[
            jax.ShapeDtypeStruct((count, n, 2 * n), jnp.float32),
            jax.ShapeDtypeStruct((count, 8, n), jnp.float32),
            jax.ShapeDtypeStruct((count, 10, n, n), jnp.float32),
            jax.ShapeDtypeStruct((2, n), jnp.float32),
        ],
        scratch_shapes=[pltpu.VMEM(own.shape, own.dtype)],
        compiler_params=pltpu.CompilerParams(vmem_limit_bytes=VMEM),
        name="slab",
    )(order, slots, total, plane, plane_rows, sandwich, own, *pieces)


def plane_products(partner_ref, picked, raw, finish):
    count = partner_ref.shape[0]
    total = jnp.zeros((1, partner_ref.shape[-1]), jnp.float32)
    for begin in range(0, count, GROUP):
        group = range(begin, min(begin + GROUP, count))
        pairs = [(partner_ref[i, 0], partner_ref[i, 1]) for i in group]
        partners = polar(pairs) if raw else [jnp.concatenate(pair, 1) for pair in pairs]
        rotated = [
            product(picked(i), both(right_form, split(partner))) for i, partner in zip(group, partners)
        ]
        for i, matrix in zip(group, rotated):
            phase, rows = column_terms(matrix)
            finish(i, matrix, rows)
            total = total + phase
    return total


def plane_kernel(order_ref, sandwich_ref, partner_ref, before_ref, out_ref, rows_ref, total_ref, *, first):
    def finish(i, matrix, rows):
        out_ref[first + i] = matrix
        store_rows(rows_ref, first + i, rows)

    total = plane_products(partner_ref, lambda i: split(sandwich_ref[order_ref[first + i]]), True, finish)
    total_ref[...] = before_ref[...]
    total_ref[0:1] = total_ref[0:1] + total


def plane_call(order, sandwich, partner, first, total):
    size, _, n, _ = partner.shape
    whole = pl.BlockSpec(memory_space=pltpu.VMEM)
    return pl.pallas_call(
        functools.partial(plane_kernel, first=first),
        in_specs=[pl.BlockSpec(memory_space=pltpu.SMEM)] + [whole] * 3,
        out_specs=[whole] * 3,
        out_shape=[
            jax.ShapeDtypeStruct((size, n, 2 * n), jnp.float32),
            jax.ShapeDtypeStruct((size, 8, n), jnp.float32),
            jax.ShapeDtypeStruct((2, n), jnp.float32),
        ],
        compiler_params=pltpu.CompilerParams(vmem_limit_bytes=VMEM),
        name="plane",
    )(order, sandwich, partner, total)


def middle_kernel(
    order_ref, sandwich_ref, partner_ref, before_ref, slab_ref, slab_rows, _, parts_ref, total_ref, last_ref, *, first
):
    size = partner_ref.shape[0]
    for i in range(last_ref.shape[1]):
        last_ref[0, i], last_ref[1, i] = split(sandwich_ref[order_ref[first + size + i]])

    def finish(i, matrix, rows):
        k = order_ref[first + i]
        combine(parts_ref, k, (matrix, slab_ref[k]), (rows, load_rows(slab_rows, k)))

    total = plane_products(partner_ref, lambda i: split(sandwich_ref[order_ref[first + i]]), False, finish)
    total_ref[...] = before_ref[...]
    total_ref[0:1] = total_ref[0:1] + total


def middle_call(order, sandwich, partner, first, total, slab, slab_rows, parts, last):
    _, n, width = sandwich.shape
    whole = pl.BlockSpec(memory_space=pltpu.VMEM)
    return pl.pallas_call(
        functools.partial(middle_kernel, first=first),
        in_specs=[pl.BlockSpec(memory_space=pltpu.SMEM)] + [whole] * 6,
        out_specs=[whole] * 3,
        out_shape=[
            jax.ShapeDtypeStruct(parts.shape, parts.dtype),
            jax.ShapeDtypeStruct(total.shape, total.dtype),
            jax.ShapeDtypeStruct((2, last, n, width), jnp.bfloat16),
        ],
        input_output_aliases={6: 0},
        compiler_params=pltpu.CompilerParams(vmem_limit_bytes=VMEM),
        name="middle",
    )(order, sandwich, partner, total, slab, slab_rows, parts)


def last_kernel(left_ref, partner_ref, before_ref, out_ref, rows_ref, total_ref):
    def finish(i, matrix, rows):
        out_ref[i] = matrix
        store_rows(rows_ref, i, rows)

    total = plane_products(partner_ref, lambda i: (left_ref[0, i], left_ref[1, i]), False, finish)
    total_ref[...] = before_ref[...]
    total_ref[0:1] = total_ref[0:1] + total


def last_call(left, partner, total):
    _, size, n, width = left.shape
    whole = pl.BlockSpec(memory_space=pltpu.VMEM)
    return pl.pallas_call(
        last_kernel,
        in_specs=[whole] * 3,
        out_specs=[whole] * 3,
        out_shape=[
            jax.ShapeDtypeStruct((size, n, width), jnp.float32),
            jax.ShapeDtypeStruct((size, 8, n), jnp.float32),
            jax.ShapeDtypeStruct(total.shape, total.dtype),
        ],
        compiler_params=pltpu.CompilerParams(vmem_limit_bytes=VMEM),
        name="last",
    )(left, partner, total)


def combine_kernel(order_ref, plane_ref, plane_rows, slab_ref, slab_rows, _, parts_ref, *, first):
    for i in range(plane_ref.shape[0]):
        k = order_ref[first + i]
        combine(
            parts_ref, k, (plane_ref[i], slab_ref[k]), (load_rows(plane_rows, i), load_rows(slab_rows, k))
        )


def combine_call(order, plane, plane_rows, slab, slab_rows, parts, first):
    whole = pl.BlockSpec(memory_space=pltpu.VMEM)
    return pl.pallas_call(
        functools.partial(combine_kernel, first=first),
        in_specs=[pl.BlockSpec(memory_space=pltpu.SMEM)] + [whole] * 5,
        out_specs=whole,
        out_shape=jax.ShapeDtypeStruct(parts.shape, parts.dtype),
        input_output_aliases={5: 0},
        compiler_params=pltpu.CompilerParams(vmem_limit_bytes=VMEM),
        name="combine",
    )(order, plane, plane_rows, slab, slab_rows, parts)


def gradient_kernel(first_ref, second_ref, parts_ref, out_ref, centres_ref, buffer, small, sems, small_sem, *, everything):
    count, _, n, _ = buffer.shape
    centres = (first_ref[...] + second_ref[...]) / (-2.0 * everything)
    small[...] = centres
    small_copy = pltpu.make_async_copy(small, centres_ref, small_sem)
    small_copy.start()
    across = [centres[d : d + 1] for d in range(2)]
    down = [jnp.broadcast_to(row, (n, n)).T for row in across]

    def copy_out(k):
        return pltpu.make_async_copy(buffer.at[k], out_ref.at[k], sems.at[k])

    @pl.loop(0, count)
    def _(k):
        real, imag = parts_ref[k, 0], parts_ref[k, 1]
        for d in range(2):
            real = real + (parts_ref[k, 2 + 4 * d] * across[d] - parts_ref[k, 4 + 4 * d] * down[d])
            imag = imag + (parts_ref[k, 3 + 4 * d] * across[d] + parts_ref[k, 5 + 4 * d] * down[d])
        for p, half in enumerate((real, imag)):
            buffer[k, p] = half
            pltpu.make_async_copy(buffer.at[k, p], out_ref.at[k, p], sems.at[k]).start()

    small_copy.wait()

    @pl.loop(0, count)
    def _(k):
        copy_out(k).wait()


def gradient_call(totals, parts, everything):
    count, _, n, _ = parts.shape
    whole = pl.BlockSpec(memory_space=pltpu.VMEM)
    return pl.pallas_call(
        functools.partial(gradient_kernel, everything=everything),
        in_specs=[whole] * 3,
        out_specs=[pl.BlockSpec(memory_space=pl.ANY)] * 2,
        out_shape=[
            jax.ShapeDtypeStruct((count, 2, n, n), jnp.float32),
            jax.ShapeDtypeStruct((2, n), jnp.float32),
        ],
        scratch_shapes=[
            pltpu.VMEM((count, 2, n, n), jnp.float32),
            pltpu.VMEM((2, n), jnp.float32),
            pltpu.SemaphoreType.DMA((count,)),
            pltpu.SemaphoreType.DMA,
        ],
        compiler_params=pltpu.CompilerParams(vmem_limit_bytes=VMEM),
        name="gradient",
    )(*totals, parts)


def shifted(value, axis, steps):
    count = lax.axis_size(axis)
    return lax.ppermute(value, axis, [(source, (source + steps) % count) for source in range(count)])


def reduce_parts(value):
    count = lax.axis_size("kxy")
    if lax.axis_size("kz") != 2 or count & (count - 1) or count < 4:
        return lax.psum(value, ("kxy", "kz")), jnp.zeros_like(value)

    def swapped(value, bits, core):
        pairs = [(2 * s + c, 2 * (s ^ bits) + (c ^ core)) for s in range(count) for c in range(2)]
        return lax.ppermute(value, ("kxy", "kz"), pairs)

    value = value + swapped(value, 0, 1) + (swapped(value, 1, 0) + swapped(value, 1, 1))
    distance = count // 2
    while distance > 2:
        value = value + swapped(value, distance, 1)
        distance //= 2
    return value, swapped(value, distance, 1)


def body(start_rotation, correlations, neighbours):
    count = start_rotation.shape[0]
    block_index = lax.axis_index("kxy") * lax.axis_size("kz") + lax.axis_index("kz")
    everything = count * lax.axis_size("kxy") * lax.axis_size("kz")
    plane_slots = neighbours[:, 0] % count
    positions = jnp.arange(count, dtype=jnp.int32)
    order = jnp.max(jnp.where(plane_slots[:, None] == positions[None], positions[:, None], 0), axis=0)
    remote = (neighbours[:, 1] // count != block_index).astype(jnp.int32)
    slab_slots = neighbours[:, 1] % count + count * remote

    partners = [shifted(take_call(start_rotation, RAW), "kxy", -2)]
    rotation, late, *parts = polar_call(start_rotation, RAW, count - RAW, GROUP, [], CHUNKS)
    partners += [shifted(part, "kxy", -2) for part in parts]
    rotation, early = polar_call(start_rotation, 0, RAW, GROUP, [rotation], ())
    from_slab = [shifted(part, "kz", -1) for part in (early, late)]
    for_plane, for_slab = sandwich_call(rotation, correlations, GROUP)
    total = jnp.zeros((2, rotation.shape[-1]), jnp.float32)
    plane, plane_rows, total = plane_call(order, for_plane, partners[0], 0, total)
    slab, slab_rows, parts, total = slab_call(
        order, slab_slots, total, plane, plane_rows, for_slab, rotation, from_slab
    )
    parts, total, for_last = middle_call(
        order, for_plane, partners[1], RAW, total, slab, slab_rows, parts, CHUNKS[-1]
    )
    plane, plane_rows, total = last_call(for_last, partners[2], total)
    totals = reduce_parts(total)
    parts = combine_call(order, plane, plane_rows, slab, slab_rows, parts, count - CHUNKS[-1])
    gradient, centres = gradient_call(totals, parts, everything)
    return (rotation, gradient, centres)


def solution(mesh):
    in_specs = (
        P(("grp", "kxy", "kz"), None, None, None),
        P(("grp", "kxy", "kz"), None, None, None, None),
        P(("grp", "kxy", "kz"), None),
    )
    out_specs = (
        P(("grp", "kxy", "kz"), None, None, None),
        P(("grp", "kxy", "kz"), None, None, None),
        P("grp", None),
    )
    return jax.shard_map(body, mesh=mesh, in_specs=in_specs, out_specs=out_specs, check_vma=False)
```
